32 devices in a mesh: parts: 2 (over y), cell: 4 (over z), grp: 4 (over x, core).
Axes of the slice: x: 2, y: 2, z: 4, core: 2. Of those that a mesh axis runs over, the one named last changes fastest.
Arguments:
- sketch: bfloat16 [98304, 256], P(('parts', 'cell', 'grp')), parts along dimension 0, may hold values from -0.27063294 to 0.27063294, as said below
- slab: bfloat16 [98304, 128], P(('parts', 'cell', 'grp')), parts along dimension 0, may hold values from -6 to 6
Outputs:
- r_factor: float32 [512, 256], P('parts'), parts along dimension 0
- basis: bfloat16 [98304, 256], P(('parts', 'cell', 'grp')), parts along dimension 0
- projected: float32 [512, 128], P(('parts', 'cell'), 'grp'), parts along dimension 0
The draws below stay inside these ranges and needn't reach their ends.
There are 2 independent parts, one for each index of `parts`. The reference program is written for one: setup_inputs(seed, part) draws one part's arguments, and reference() takes and returns one part's arrays. A program takes and returns all parts, laid end to end along the dimension named above; each array names one. Nothing has to cross between parts.
Inputs may be any that keep to these rules, and one draw needn't show every extreme that they name: A scaled random sketch of full column rank.
All inputs are finite; a program needn't handle non-finite values.
Results may differ from the reference program's by a relative error of at most 0.001.
Values sent between devices are 32-bit elements; how exact they have to be, the bound alone decides.
A program may use at most 64 MiB of HBM per device.

```python
import jax
import jax.numpy as jnp
from jax import lax

ROW_DEV = 3072
K = 256
SLAB = 128
ROWS = 49152


def draw_sketch(key, part):
    key_base, key_rows, key_cols = jax.random.split(jax.random.fold_in(key, 17), 3)
    positions = jnp.arange(ROWS, dtype=jnp.float32)
    trend = 1.0 + 2.0 * positions / ROWS
    row_scale = jnp.exp(jax.random.uniform(key_rows, (ROWS,), jnp.float32, 0.0, jnp.log(10.0)))
    col_scale = jnp.exp(jax.random.uniform(key_cols, (K,), jnp.float32, jnp.log(0.5), jnp.log(2.0)))
    base = jnp.clip(jax.random.normal(key_base, (ROWS, K), jnp.float32), -4.0, 4.0)
    values = base * (row_scale * trend)[:, None] * col_scale[None, :] / (4.0 * jnp.sqrt(ROWS * 1.0))
    return values.astype(jnp.bfloat16)


def levels(stream_key, shape, cuts, low, largest):
    level = 1.0
    for position, blocks in cuts:
        steps = jax.random.uniform(jax.random.fold_in(jax.random.fold_in(stream_key, 6), position), (blocks,), jnp.float32, low / len(cuts), largest / len(cuts))
        level = level * jnp.repeat(jnp.exp(steps), shape[position] // blocks).reshape((-1,) + (1,) * (len(shape) - 1 - position))
    return level


def gaussian(key, dims, deviation, limit, shards=(), kind=jnp.bfloat16):
    values = jax.random.normal(key, dims, jnp.float32) * deviation
    if len(shards) > 0:
        values = levels(key, dims, shards, -0.22, 0.18) * values
    return jnp.clip(values, min=-limit, max=limit).astype(kind)


def setup_inputs(seed: int = 0, part: int = 0) -> dict:
    arg_keys = jax.random.split(jax.random.key(seed), 3)
    part_keys = jax.random.split(jax.random.fold_in(arg_keys[2], part), 3)
    sketch = draw_sketch(jax.random.fold_in(jax.random.fold_in(arg_keys[2], part), 71), part)
    slab = gaussian(part_keys[1], (ROWS, SLAB), 1.0, 6.0, ((0, 16),))
    return {"sketch": sketch, "slab": slab}


def gram_of(piece):
    return lax.dot_general(piece.astype(jnp.float32), piece.astype(jnp.float32), (((0,), (0,)), ((), ())), preferred_element_type=jnp.float32)

def reference(sketch, slab):
    sketch_blocks = sketch.reshape(ROWS // ROW_DEV, ROW_DEV, K)
    slab_blocks = slab.reshape(ROWS // ROW_DEV, ROW_DEV, SLAB)

    def add_stats(totals, pieces):
        rows_block, slab_block = pieces
        gram_part = gram_of(rows_block)
        cross_part = lax.dot_general(rows_block.astype(jnp.float32), slab_block.astype(jnp.float32), (((0,), (0,)), ((), ())), preferred_element_type=jnp.float32)
        return ((totals[0] + gram_part, totals[1] + cross_part), None)
    start_totals = (jnp.zeros((K, K), jnp.float32), jnp.zeros((K, SLAB), jnp.float32))
    totals, unused = lax.scan(add_stats, start_totals, (sketch_blocks, slab_blocks))
    gram_sum, cross_sum = totals
    lower_factor = jnp.linalg.cholesky(gram_sum)
    identity = jnp.eye(K, dtype=jnp.float32)
    inverse_lower = lax.linalg.triangular_solve(lower_factor, identity, left_side=True, lower=True)
    inverse_upper = inverse_lower.T

    def solve_block(rows_block):
        exact_rows = jnp.dot(rows_block.astype(jnp.float32), inverse_upper.astype(jnp.float32), precision=lax.Precision.HIGHEST, preferred_element_type=jnp.float32)
        return exact_rows.astype(jnp.bfloat16)
    basis = lax.map(solve_block, sketch_blocks).reshape(ROWS, K)
    projected = lax.linalg.triangular_solve(lower_factor, cross_sum, left_side=True, lower=True)
    return (lower_factor.T, basis, projected)
```

```python
import functools

import jax
import jax.numpy as jnp
from jax import lax
from jax.experimental import pallas as pl
from jax.experimental.pallas import tpu as pltpu
from jax.sharding import PartitionSpec as P

SUB = 8
CORES = 2
FACTOR_VMEM = 64_500_000
BASIS_VMEM = 20 * 2**20
SUM_STEP = 768
BASIS_STEP = 512
HIGHEST = lax.Precision.HIGHEST


def dot(a, b, contract, precision=None):
    return lax.dot_general(
        a, b, (contract, ((), ())), precision=precision, preferred_element_type=jnp.float32
    )


def chunks_of(total, step):
    return [pl.ds(start, min(step, total - start)) for start in range(0, total, step)]


def sums_over(a_ref, b_ref, loads):
    total = None
    for rows, load in loads:
        load.wait()
        part = dot(a_ref[rows, :], b_ref[rows, :], ((0,), (0,)))
        total = part if total is None else total + part
    return total


def tree(terms):
    while len(terms) > 1:
        terms = [a + b for a, b in zip(terms[::2], terms[1::2])]
    return terms[0]


def factor_base(block, ones_ref):
    n = block.shape[0]
    shape = (SUB, 2 * n)
    ones = ones_ref[:, : 2 * n]
    tiles = n // SUB
    sub = lax.broadcasted_iota(jnp.int32, shape, 0)
    lane = lax.broadcasted_iota(jnp.int32, shape, 1)
    eye = jnp.where(
        lax.broadcasted_iota(jnp.int32, (n, n), 0) == lax.broadcasted_iota(jnp.int32, (n, n), 1), 1.0, 0.0)
    wide = jnp.concatenate([block, eye.astype(jnp.float32)], axis=1)
    m = [wide[q * SUB : (q + 1) * SUB, :] for q in range(tiles)]
    done = []

    def row(x, j):
        return jnp.broadcast_to(x[j : j + 1, :], shape)

    def col(x, j):
        return jnp.broadcast_to(x[:, j : j + 1], shape)

    for p in range(tiles):
        t = m[p]
        c = [col(t, p * SUB + i) * ones for i in range(SUB)]
        s = {(j, i): row(c[i], j) for i in range(SUB) for j in range(i + 1)}
        r = jnp.zeros(shape, jnp.float32)
        for j in range(SUB):
            at = sub == j
            pivot = s[j, j]
            inv, root = 1.0 / pivot, lax.rsqrt(pivot)
            f = jnp.where(at, -inv, c[j] * inv)
            t_j = row(t, j)
            r = jnp.where(at, t_j * root, r)
            t = jnp.where(at, 0.0, t) - f * t_j
            scaled = {i: s[j, i] * inv for i in range(j + 1, SUB)}
            for i in range(j + 1, SUB):
                c[i] = jnp.where(at, 0.0, c[i]) - f * s[j, i]
                for h in range(j + 1, i + 1):
                    s[h, i] = s[h, i] - scaled[h] * s[j, i]
        done.append(jnp.where((lane >= sub + p * SUB), r, 0.0))
        if p + 1 < tiles:
            rows = [row(t, i) for i in range(SUB)]
            later = range(p + 1, tiles)
            terms = [[col(m[q], p * SUB + i) * rows[i] for q in later] for i in range(SUB)]
            for at, q in enumerate(later):
                m[q] = m[q] - tree([terms[i][at] for i in range(SUB)])
    done = jnp.concatenate(done, axis=0)
    return done[:, :n], done[:, n:]


def extend(r11, w11, g12, g22, ones_ref):
    h = r11.shape[0]
    r12 = dot(w11, g12, ((1,), (0,)), HIGHEST)
    r21 = r12.T
    r22, w22 = factor_base(g22 - dot(r21, r12, ((1,), (0,)), HIGHEST), ones_ref)
    w21 = -dot(w22, dot(r21, w11, ((1,), (0,)), HIGHEST), ((1,), (0,)), HIGHEST)
    zero = jnp.zeros((h, h), jnp.float32)
    return (
        jnp.concatenate([jnp.concatenate([r11, r12], axis=1), jnp.concatenate([zero, r22], axis=1)], axis=0),
        jnp.concatenate([jnp.concatenate([w11, zero], axis=1), jnp.concatenate([w21, w22], axis=1)], axis=0),
    )


def factor_kernel(
    cells, grps, sketch_hbm, slab_hbm, r_ref, inv_ref, cross_ref, sketch_ref,
    slab_ref, sketch_sems, slab_sems, ones_ref,
    own_a, core_a, chip_a, all_a, own_b, core_b, chip_b, all_b,
    own_c, grp_c, cell_c, all_c, own_x, grp_x, cell_x,
    core_send, core_recv, a_send, a_recv, b_send, b_recv, gc_send, gc_recv, zc_send, zc_recv,
    ac_send, ac_recv, gx_send, gx_recv, zx_send, zx_recv,
):
    def loading(source, target, sems):
        loads = []
        for i, rows in enumerate(chunks_of(source.shape[0], SUM_STEP)):
            load = pltpu.make_async_copy(source.at[rows, :], target.at[rows, :], sems.at[i])
            load.start()
            loads.append((rows, load))
        return loads

    sketch_loads = loading(sketch_hbm, sketch_ref, sketch_sems)
    slab_loads = loading(slab_hbm, slab_ref, slab_sems)
    me_c = lax.axis_index("cell")
    me_g = lax.axis_index("grp")
    chips_x = grps // CORES
    me_x, core = lax.div(me_g, CORES), lax.rem(me_g, CORES)
    me_chip = me_c * chips_x + me_x
    other = me_x * CORES + (1 - core)
    half = own_b.shape[1]
    quarter = half // 2
    started = []

    def send(source, target, send_sem, recv_sem, device):
        copy = pltpu.make_async_remote_copy(
            src_ref=source, dst_ref=target, send_sem=send_sem, recv_sem=recv_sem,
            device_id=device, device_id_type=pl.DeviceIdType.MESH)
        copy.start()
        started.append(copy)
        return copy

    def rows_of(ref, index, count):
        return ref.at[pl.ds(pl.multiple_of(index * count, SUB), count), :]

    grp_peers = [{"grp": lax.rem(me_g + d, grps)} for d in range(1, grps)]
    cell_peers = [{"cell": lax.rem(me_c + d, cells)} for d in range(1, cells)]
    chip_peers = [
        {"cell": lax.rem(me_c + dc, cells), "grp": lax.rem(me_x + dx, chips_x) * CORES + core}
        for dx in reversed(range(chips_x)) for dc in sorted(range(cells), key=lambda d: -min(d, cells - d)) if dc or dx]

    barrier = pltpu.get_barrier_semaphore()
    beyond = [{"cell": peer["cell"], "grp": peer["grp"]} for peer in chip_peers]
    for peer in beyond + [p for d, p in enumerate(grp_peers, 1)]:
        pl.semaphore_signal(barrier, inc=1, device_id=peer, device_id_type=pl.DeviceIdType.MESH)

    gram = sums_over(sketch_ref, sketch_ref, sketch_loads)
    eighth = quarter // 2
    own_a[...] = jnp.concatenate([gram[:eighth, :quarter], gram[eighth:quarter, :quarter]], axis=1)
    own_b[...] = jnp.concatenate([gram[:quarter, quarter:half], gram[quarter:half, quarter:half]], axis=1)
    pl.semaphore_wait(barrier, len(beyond) + len(grp_peers))

    def halves(own, landing, index):
        count = own.shape[0] // CORES
        return send(rows_of(own, 1 - core, count), landing, core_send.at[index], core_recv.at[index], {"grp": other})

    a1 = halves(own_a, core_a, 0)
    b1 = halves(own_b, core_b, 1)
    own_c[0:half, :] = gram[:half, half:]
    own_c[half:, :] = gram[half:, half:]

    def to_grps(own, landing, send_sems, recv_sems):
        count = own.shape[0] // grps
        return [
            send(rows_of(own, peer["grp"], count), landing.at[i], send_sems.at[i], recv_sems.at[i], peer)
            for i, peer in enumerate(grp_peers)]

    def sum_grps(copies, own, landing, slots):
        count = own.shape[0] // grps
        for copy in copies:
            copy.wait_recv()
        slots[me_c] = tree([own[pl.ds(pl.multiple_of(me_g * count, SUB), count), :]] + [landing[i] for i in range(grps - 1)])

    def spread(slots, me, peers, send_sems, recv_sems):
        return [send(slots.at[me], slots.at[me], send_sems.at[i], recv_sems.at[i], peer) for i, peer in enumerate(peers)]

    def sum_slots(copies, slots):
        for copy in copies:
            copy.wait_recv()
        return tree([slots[i] for i in range(slots.shape[0])])

    c1 = to_grps(own_c, grp_c, gc_send, gc_recv)

    def chip_sum(copy, own, landing, slots, send_sems, recv_sems):
        count = own.shape[0] // CORES
        copy.wait_recv()
        slots[me_chip] = own[pl.ds(pl.multiple_of(core * count, SUB), count), :] + landing[...]
        return spread(slots, me_chip, chip_peers, send_sems, recv_sems)

    a2 = chip_sum(a1, own_a, core_a, chip_a, a_send, a_recv)
    b2 = chip_sum(b1, own_b, core_b, chip_b, b_send, b_recv)

    cross = sums_over(slab_ref, sketch_ref, slab_loads)
    days = cross.shape[0] // grps
    for g in range(grps):
        own_x[2 * g * days : (2 * g + 1) * days, :] = cross[g * days : (g + 1) * days, :half]
        own_x[(2 * g + 1) * days : 2 * (g + 1) * days, :] = cross[g * days : (g + 1) * days, half:]

    sum_grps(c1, own_c, grp_c, cell_c)
    c2 = spread(cell_c, me_c, cell_peers, zc_send, zc_recv)

    def both(copies, slots, target, index):
        target[core] = sum_slots(copies, slots)
        return send(target.at[core], target.at[core], core_send.at[index], core_recv.at[index], {"grp": other})

    a3 = both(a2, chip_a, all_a, 2)
    b3 = both(b2, chip_b, all_b, 3)
    x1 = to_grps(own_x, grp_x, gx_send, gx_recv)
    ones_ref[...] = jnp.ones_like(ones_ref)

    a3.wait_recv()
    packed = jnp.concatenate([all_a[i] for i in range(CORES)], axis=0)
    first = jnp.concatenate([packed[:, :quarter], packed[:, quarter:]], axis=0)
    r_00, w_00 = factor_base(first, ones_ref)

    count = own_c.shape[0] // grps
    all_c[pl.ds(pl.multiple_of(me_g * count, SUB), count), :] = sum_slots(c2, cell_c)
    c3 = [
        send(rows_of(all_c, me_g, count), rows_of(all_c, me_g, count), ac_send.at[i], ac_recv.at[i], peer)
        for i, peer in enumerate(grp_peers)]

    b3.wait_recv()
    packed = jnp.concatenate([all_b[i] for i in range(CORES)], axis=0)
    r11, w11 = extend(r_00, w_00, packed[:, :quarter], packed[:, quarter:], ones_ref)
    zero = jnp.zeros((half, half), jnp.float32)
    r_ref[0:half, 0:half] = r11
    r_ref[half:, 0:half] = zero
    inv_ref[0:half, 0:half] = w11
    inv_ref[0:half, half:] = zero

    sum_grps(x1, own_x, grp_x, cell_x)
    x2 = spread(cell_x, me_c, cell_peers, zx_send, zx_recv)

    for copy in c3:
        copy.wait_recv()
    r12 = dot(w11, all_c[0:half, :], ((1,), (0,)), HIGHEST)
    r21 = r12.T
    rest = all_c[half:, :] - dot(r21, r12, ((1,), (0,)), HIGHEST)
    mixed = dot(r21, w11, ((1,), (0,)), HIGHEST)
    r_ref[0:half, half:] = r12
    r_00, w_00 = factor_base(rest[:quarter, :quarter], ones_ref)
    r22, w22 = extend(r_00, w_00, rest[:quarter, quarter:], rest[quarter:, quarter:], ones_ref)
    r_ref[half:, half:] = r22
    inv_ref[half:, 0:half] = -dot(w22, mixed, ((1,), (0,)), HIGHEST)
    inv_ref[half:, half:] = w22
    cross_ref[...] = sum_slots(x2, cell_x)
    for copy in started:
        copy.wait_send()


def factored(sketch, slab, cells, grps):
    k, days = sketch.shape[1], slab.shape[1]
    half, quarter = k // 2, k // 4
    chips = cells * grps // CORES
    f32 = jnp.float32
    dma = pltpu.SemaphoreType.DMA
    a_rows, b_rows, c_rows, x_rows = quarter // 2, quarter, 2 * half, 2 * days
    assert grps % CORES == 0 and cells > 1 and k % (8 * SUB) == 0
    assert c_rows % (SUB * grps) == 0 and x_rows % (2 * SUB * grps) == 0

    def small(rows):
        part = rows // CORES
        return [pltpu.VMEM((rows, half), f32), pltpu.VMEM((part, half), f32),
                pltpu.VMEM((chips, part, half), f32), pltpu.VMEM((CORES, part, half), f32)]

    def large(rows):
        part = rows // grps
        return [pltpu.VMEM((rows, half), f32), pltpu.VMEM((grps - 1, part, half), f32),
                pltpu.VMEM((cells, part, half), f32)]

    return pl.pallas_call(
        functools.partial(factor_kernel, cells, grps),
        out_shape=(
            jax.ShapeDtypeStruct((k, k), f32),
            jax.ShapeDtypeStruct((k, k), f32),
            jax.ShapeDtypeStruct((x_rows // grps, half), f32),
            jax.ShapeDtypeStruct(sketch.shape, sketch.dtype),
        ),
        in_specs=[pl.BlockSpec(memory_space=pltpu.HBM)] * 2,
        out_specs=(pl.BlockSpec(memory_space=pltpu.VMEM),) * 4,
        scratch_shapes=[
            pltpu.VMEM(slab.shape, slab.dtype),
            dma((len(chunks_of(sketch.shape[0], SUM_STEP)),)),
            dma((len(chunks_of(slab.shape[0], SUM_STEP)),)),
            pltpu.VMEM((SUB, k), f32),
        ] + small(a_rows) + small(b_rows) + large(c_rows) + [pltpu.VMEM((c_rows, half), f32)] + large(x_rows)
        + [dma((4,))] * 2 + [dma((chips - 1,))] * 4
        + [dma((grps - 1,))] * 2 + [dma((cells - 1,))] * 2 + [dma((grps - 1,))] * 4 + [dma((cells - 1,))] * 2,
        compiler_params=pltpu.CompilerParams(collective_id=0, has_side_effects=True, vmem_limit_bytes=FACTOR_VMEM),
        name="reduce_and_factor",
    )(sketch, slab)


def basis_kernel(
    r_in, inv_ref, cross_ref, sketch_ref, r_out, basis_hbm, proj_ref, basis_ref, store_sems,
):
    steps = chunks_of(sketch_ref.shape[0], BASIS_STEP)
    half = cross_ref.shape[1]
    days = cross_ref.shape[0] // 2
    r_out[...] = r_in[...]
    whole = inv_ref[...]
    high = whole.astype(jnp.bfloat16)
    low = (whole - high.astype(jnp.float32)).astype(jnp.bfloat16)
    stores = []
    for i, rows in enumerate(steps):
        part = sketch_ref[rows, :]
        exact = dot(part, high, ((1,), (1,))) + dot(part, low, ((1,), (1,)))
        basis_ref[rows, :] = exact.astype(jnp.bfloat16)
        stores.append(pltpu.make_async_copy(basis_ref.at[rows, :], basis_hbm.at[rows, :], store_sems.at[i]))
        stores[-1].start()
    count = proj_ref.shape[1]
    mine = inv_ref[pl.ds(pl.multiple_of(lax.axis_index("cell") * count, SUB), count), :]
    proj_ref[...] = dot(cross_ref[0:days, :], mine[:, :half], ((1,), (1,)), HIGHEST) + dot(
        cross_ref[days:, :], mine[:, half:], ((1,), (1,)), HIGHEST)
    for store in stores:
        store.wait()


def local(cells, grps, sketch, slab):
    k, days = sketch.shape[1], slab.shape[1]
    r_in, inverse, cross, held = factored(sketch, slab, cells, grps)
    vmem = pl.BlockSpec(memory_space=pltpu.VMEM)
    hbm = pl.BlockSpec(memory_space=pl.ANY)
    steps = len(chunks_of(sketch.shape[0], BASIS_STEP))
    r_factor, basis, projected = pl.pallas_call(
        basis_kernel,
        out_shape=(
            jax.ShapeDtypeStruct((k, k), jnp.float32),
            jax.ShapeDtypeStruct(sketch.shape, jnp.bfloat16),
            jax.ShapeDtypeStruct((days // grps, k // cells), jnp.float32),
        ),
        in_specs=[vmem] * 4,
        out_specs=(vmem, hbm, vmem),
        scratch_shapes=[
            pltpu.VMEM(sketch.shape, jnp.bfloat16),
            pltpu.SemaphoreType.DMA((steps,)),
        ],
        compiler_params=pltpu.CompilerParams(vmem_limit_bytes=BASIS_VMEM),
        name="basis",
    )(r_in, inverse, cross, held)
    return r_factor, basis, projected.T


def solution(mesh):
    cells, grps = mesh.shape["cell"], mesh.shape["grp"]
    in_specs = (P(("parts", "cell", "grp"), None), P(("parts", "cell", "grp"), None))
    out_specs = (P("parts", None), P(("parts", "cell", "grp"), None), P(("parts", "cell"), "grp"))
    return jax.shard_map(
        functools.partial(local, cells, grps), mesh=mesh, in_specs=in_specs, out_specs=out_specs, check_vma=False)
```

```python
import functools

import jax
import jax.numpy as jnp
from jax import lax
from jax.experimental import pallas as pl
from jax.experimental.pallas import tpu as pltpu
from jax.sharding import PartitionSpec as P

SUB = 8
CORES = 2
VMEM_LIMIT = 20 * 2**20
SUM_STEP = 768
BASIS_STEP = 512
HIGHEST = lax.Precision.HIGHEST


def dot(a, b, contract, precision=None):
    return lax.dot_general(
        a, b, (contract, ((), ())), precision=precision, preferred_element_type=jnp.float32
    )


def chunks_of(total, step):
    return [pl.ds(start, min(step, total - start)) for start in range(0, total, step)]


def sums_over(a_ref, b_ref, loads):
    total = None
    for rows, load in loads:
        load.wait()
        part = dot(a_ref[rows, :], b_ref[rows, :], ((0,), (0,)))
        total = part if total is None else total + part
    return total


def tree(terms):
    while len(terms) > 1:
        terms = [a + b for a, b in zip(terms[::2], terms[1::2])]
    return terms[0]


def factor_base(block, ones_ref):
    n = block.shape[0]
    shape = (SUB, 2 * n)
    ones = ones_ref[:, : 2 * n]
    tiles = n // SUB
    sub = lax.broadcasted_iota(jnp.int32, shape, 0)
    lane = lax.broadcasted_iota(jnp.int32, shape, 1)
    eye = jnp.where(
        lax.broadcasted_iota(jnp.int32, (n, n), 0) == lax.broadcasted_iota(jnp.int32, (n, n), 1), 1.0, 0.0)
    wide = jnp.concatenate([block, eye.astype(jnp.float32)], axis=1)
    m = [wide[q * SUB : (q + 1) * SUB, :] for q in range(tiles)]
    done = []

    def row(x, j):
        return jnp.broadcast_to(x[j : j + 1, :], shape)

    def col(x, j):
        return jnp.broadcast_to(x[:, j : j + 1], shape)

    for p in range(tiles):
        t = m[p]
        c = [col(t, p * SUB + i) * ones for i in range(SUB)]
        s = {(j, i): row(c[i], j) for i in range(SUB) for j in range(i + 1)}
        r = jnp.zeros(shape, jnp.float32)
        for j in range(SUB):
            at = sub == j
            pivot = s[j, j]
            inv, root = 1.0 / pivot, lax.rsqrt(pivot)
            f = jnp.where(at, -inv, c[j] * inv)
            t_j = row(t, j)
            r = jnp.where(at, t_j * root, r)
            t = jnp.where(at, 0.0, t) - f * t_j
            scaled = {i: s[j, i] * inv for i in range(j + 1, SUB)}
            for i in range(j + 1, SUB):
                c[i] = jnp.where(at, 0.0, c[i]) - f * s[j, i]
                for h in range(j + 1, i + 1):
                    s[h, i] = s[h, i] - scaled[h] * s[j, i]
        done.append(jnp.where((lane >= sub + p * SUB), r, 0.0))
        if p + 1 < tiles:
            rows = [row(t, i) for i in range(SUB)]
            later = range(p + 1, tiles)
            terms = [[col(m[q], p * SUB + i) * rows[i] for q in later] for i in range(SUB)]
            for at, q in enumerate(later):
                m[q] = m[q] - tree([terms[i][at] for i in range(SUB)])
    done = jnp.concatenate(done, axis=0)
    return done[:, :n], done[:, n:]


def extend(r11, w11, g12, g22, ones_ref):
    h = r11.shape[0]
    r12 = dot(w11, g12, ((1,), (0,)), HIGHEST)
    r21 = r12.T
    r22, w22 = factor_base(g22 - dot(r21, r12, ((1,), (0,)), HIGHEST), ones_ref)
    w21 = -dot(w22, dot(r21, w11, ((1,), (0,)), HIGHEST), ((1,), (0,)), HIGHEST)
    zero = jnp.zeros((h, h), jnp.float32)
    return (
        jnp.concatenate([jnp.concatenate([r11, r12], axis=1), jnp.concatenate([zero, r22], axis=1)], axis=0),
        jnp.concatenate([jnp.concatenate([w11, zero], axis=1), jnp.concatenate([w21, w22], axis=1)], axis=0),
    )


def factor_kernel(
    cells, grps, sketch_hbm, slab_hbm, r_ref, inv_ref, cross_ref, sketch_ref,
    slab_ref, sketch_sems, slab_sems, ones_ref,
    own_a, core_a, chip_a, all_a, own_b, core_b, chip_b, all_b,
    own_c, grp_c, cell_c, all_c, own_x, grp_x, cell_x,
    core_send, core_recv, a_send, a_recv, b_send, b_recv, gc_send, gc_recv, zc_send, zc_recv,
    ac_send, ac_recv, gx_send, gx_recv, zx_send, zx_recv,
):
    def loading(source, target, sems):
        loads = []
        for i, rows in enumerate(chunks_of(source.shape[0], SUM_STEP)):
            load = pltpu.make_async_copy(source.at[rows, :], target.at[rows, :], sems.at[i])
            load.start()
            loads.append((rows, load))
        return loads

    sketch_loads = loading(sketch_hbm, sketch_ref, sketch_sems)
    slab_loads = loading(slab_hbm, slab_ref, slab_sems)
    me_c = lax.axis_index("cell")
    me_g = lax.axis_index("grp")
    chips_x = grps // CORES
    me_x, core = lax.div(me_g, CORES), lax.rem(me_g, CORES)
    me_chip = me_c * chips_x + me_x
    other = me_x * CORES + (1 - core)
    half = own_b.shape[1]
    quarter = half // 2
    started = []

    def send(source, target, send_sem, recv_sem, device):
        copy = pltpu.make_async_remote_copy(
            src_ref=source, dst_ref=target, send_sem=send_sem, recv_sem=recv_sem,
            device_id=device, device_id_type=pl.DeviceIdType.MESH)
        copy.start()
        started.append(copy)
        return copy

    def rows_of(ref, index, count):
        return ref.at[pl.ds(pl.multiple_of(index * count, SUB), count), :]

    grp_peers = [{"grp": lax.rem(me_g + d, grps)} for d in range(1, grps)]
    cell_peers = [{"cell": lax.rem(me_c + d, cells)} for d in range(1, cells)]
    chip_peers = [
        {"cell": lax.rem(me_c + dc, cells), "grp": lax.rem(me_x + dx, chips_x) * CORES + core}
        for dx in reversed(range(chips_x)) for dc in sorted(range(cells), key=lambda d: -min(d, cells - d)) if dc or dx]

    barrier = pltpu.get_barrier_semaphore()
    beyond = [{"cell": peer["cell"], "grp": peer["grp"]} for peer in chip_peers]
    for peer in beyond + [p for d, p in enumerate(grp_peers, 1)]:
        pl.semaphore_signal(barrier, inc=1, device_id=peer, device_id_type=pl.DeviceIdType.MESH)

    gram = sums_over(sketch_ref, sketch_ref, sketch_loads)
    eighth = quarter // 2
    own_a[...] = jnp.concatenate([gram[:eighth, :quarter], gram[eighth:quarter, :quarter]], axis=1)
    own_b[...] = jnp.concatenate([gram[:quarter, quarter:half], gram[quarter:half, quarter:half]], axis=1)
    pl.semaphore_wait(barrier, len(beyond) + len(grp_peers))

    def halves(own, landing, index):
        count = own.shape[0] // CORES
        return send(rows_of(own, 1 - core, count), landing, core_send.at[index], core_recv.at[index], {"grp": other})

    a1 = halves(own_a, core_a, 0)
    b1 = halves(own_b, core_b, 1)
    own_c[0:half, :] = gram[:half, half:]
    own_c[half:, :] = gram[half:, half:]

    def to_grps(own, landing, send_sems, recv_sems):
        count = own.shape[0] // grps
        return [
            send(rows_of(own, peer["grp"], count), landing.at[i], send_sems.at[i], recv_sems.at[i], peer)
            for i, peer in enumerate(grp_peers)]

    def sum_grps(copies, own, landing, slots):
        count = own.shape[0] // grps
        for copy in copies:
            copy.wait_recv()
        slots[me_c] = tree([own[pl.ds(pl.multiple_of(me_g * count, SUB), count), :]] + [landing[i] for i in range(grps - 1)])

    def spread(slots, me, peers, send_sems, recv_sems):
        return [send(slots.at[me], slots.at[me], send_sems.at[i], recv_sems.at[i], peer) for i, peer in enumerate(peers)]

    def sum_slots(copies, slots):
        for copy in copies:
            copy.wait_recv()
        return tree([slots[i] for i in range(slots.shape[0])])

    c1 = to_grps(own_c, grp_c, gc_send, gc_recv)

    def chip_sum(copy, own, landing, slots, send_sems, recv_sems):
        count = own.shape[0] // CORES
        copy.wait_recv()
        slots[me_chip] = own[pl.ds(pl.multiple_of(core * count, SUB), count), :] + landing[...]
        return spread(slots, me_chip, chip_peers, send_sems, recv_sems)

    a2 = chip_sum(a1, own_a, core_a, chip_a, a_send, a_recv)
    b2 = chip_sum(b1, own_b, core_b, chip_b, b_send, b_recv)

    cross = sums_over(slab_ref, sketch_ref, slab_loads)
    days = cross.shape[0] // grps
    for g in range(grps):
        own_x[2 * g * days : (2 * g + 1) * days, :] = cross[g * days : (g + 1) * days, :half]
        own_x[(2 * g + 1) * days : 2 * (g + 1) * days, :] = cross[g * days : (g + 1) * days, half:]

    sum_grps(c1, own_c, grp_c, cell_c)
    c2 = spread(cell_c, me_c, cell_peers, zc_send, zc_recv)

    def both(copies, slots, target, index):
        target[core] = sum_slots(copies, slots)
        return send(target.at[core], target.at[core], core_send.at[index], core_recv.at[index], {"grp": other})

    a3 = both(a2, chip_a, all_a, 2)
    b3 = both(b2, chip_b, all_b, 3)
    x1 = to_grps(own_x, grp_x, gx_send, gx_recv)
    ones_ref[...] = jnp.ones_like(ones_ref)

    a3.wait_recv()
    packed = jnp.concatenate([all_a[i] for i in range(CORES)], axis=0)
    first = jnp.concatenate([packed[:, :quarter], packed[:, quarter:]], axis=0)
    r_00, w_00 = factor_base(first, ones_ref)

    count = own_c.shape[0] // grps
    all_c[pl.ds(pl.multiple_of(me_g * count, SUB), count), :] = sum_slots(c2, cell_c)
    c3 = [
        send(rows_of(all_c, me_g, count), rows_of(all_c, me_g, count), ac_send.at[i], ac_recv.at[i], peer)
        for i, peer in enumerate(grp_peers)]

    b3.wait_recv()
    packed = jnp.concatenate([all_b[i] for i in range(CORES)], axis=0)
    r11, w11 = extend(r_00, w_00, packed[:, :quarter], packed[:, quarter:], ones_ref)
    zero = jnp.zeros((half, half), jnp.float32)
    r_ref[0:half, 0:half] = r11
    r_ref[half:, 0:half] = zero
    inv_ref[0:half, 0:half] = w11
    inv_ref[0:half, half:] = zero

    sum_grps(x1, own_x, grp_x, cell_x)
    x2 = spread(cell_x, me_c, cell_peers, zx_send, zx_recv)

    for copy in c3:
        copy.wait_recv()
    r12 = dot(w11, all_c[0:half, :], ((1,), (0,)), HIGHEST)
    r21 = r12.T
    rest = all_c[half:, :] - dot(r21, r12, ((1,), (0,)), HIGHEST)
    mixed = dot(r21, w11, ((1,), (0,)), HIGHEST)
    r_ref[0:half, half:] = r12
    r_00, w_00 = factor_base(rest[:quarter, :quarter], ones_ref)
    r22, w22 = extend(r_00, w_00, rest[:quarter, quarter:], rest[quarter:, quarter:], ones_ref)
    r_ref[half:, half:] = r22
    inv_ref[half:, 0:half] = -dot(w22, mixed, ((1,), (0,)), HIGHEST)
    inv_ref[half:, half:] = w22
    cross_ref[...] = sum_slots(x2, cell_x)
    for copy in started:
        copy.wait_send()


def factored(sketch, slab, cells, grps):
    k, days = sketch.shape[1], slab.shape[1]
    half, quarter = k // 2, k // 4
    chips = cells * grps // CORES
    f32 = jnp.float32
    dma = pltpu.SemaphoreType.DMA
    a_rows, b_rows, c_rows, x_rows = quarter // 2, quarter, 2 * half, 2 * days
    assert grps % CORES == 0 and cells > 1 and k % (8 * SUB) == 0
    assert c_rows % (SUB * grps) == 0 and x_rows % (2 * SUB * grps) == 0

    def small(rows):
        part = rows // CORES
        return [pltpu.VMEM((rows, half), f32), pltpu.VMEM((part, half), f32),
                pltpu.VMEM((chips, part, half), f32), pltpu.VMEM((CORES, part, half), f32)]

    def large(rows):
        part = rows // grps
        return [pltpu.VMEM((rows, half), f32), pltpu.VMEM((grps - 1, part, half), f32),
                pltpu.VMEM((cells, part, half), f32)]

    return pl.pallas_call(
        functools.partial(factor_kernel, cells, grps),
        out_shape=(
            jax.ShapeDtypeStruct((k, k), f32),
            jax.ShapeDtypeStruct((k, k), f32),
            jax.ShapeDtypeStruct((x_rows // grps, half), f32),
            jax.ShapeDtypeStruct(sketch.shape, sketch.dtype),
        ),
        in_specs=[pl.BlockSpec(memory_space=pltpu.HBM)] * 2,
        out_specs=(pl.BlockSpec(memory_space=pltpu.VMEM),) * 4,
        scratch_shapes=[
            pltpu.VMEM(slab.shape, slab.dtype),
            dma((len(chunks_of(sketch.shape[0], SUM_STEP)),)),
            dma((len(chunks_of(slab.shape[0], SUM_STEP)),)),
            pltpu.VMEM((SUB, k), f32),
        ] + small(a_rows) + small(b_rows) + large(c_rows) + [pltpu.VMEM((c_rows, half), f32)] + large(x_rows)
        + [dma((4,))] * 2 + [dma((chips - 1,))] * 4
        + [dma((grps - 1,))] * 2 + [dma((cells - 1,))] * 2 + [dma((grps - 1,))] * 4 + [dma((cells - 1,))] * 2,
        compiler_params=pltpu.CompilerParams(collective_id=0, has_side_effects=True, vmem_limit_bytes=VMEM_LIMIT),
        name="reduce_and_factor",
    )(pltpu.with_memory_space_constraint(sketch, pltpu.HBM), pltpu.with_memory_space_constraint(slab, pltpu.HBM))


def basis_kernel(
    r_in, inv_ref, cross_ref, sketch_ref, r_out, basis_hbm, proj_ref, basis_ref, store_sems,
):
    steps = chunks_of(sketch_ref.shape[0], BASIS_STEP)
    half = cross_ref.shape[1]
    days = cross_ref.shape[0] // 2
    r_out[...] = r_in[...]
    whole = inv_ref[...]
    high = whole.astype(jnp.bfloat16)
    low = (whole - high.astype(jnp.float32)).astype(jnp.bfloat16)
    stores = []
    for i, rows in enumerate(steps):
        part = sketch_ref[rows, :]
        exact = dot(part, high, ((1,), (1,))) + dot(part, low, ((1,), (1,)))
        basis_ref[rows, :] = exact.astype(jnp.bfloat16)
        stores.append(pltpu.make_async_copy(basis_ref.at[rows, :], basis_hbm.at[rows, :], store_sems.at[i]))
        stores[-1].start()
    count = proj_ref.shape[1]
    mine = inv_ref[pl.ds(pl.multiple_of(lax.axis_index("cell") * count, SUB), count), :]
    proj_ref[...] = dot(cross_ref[0:days, :], mine[:, :half], ((1,), (1,)), HIGHEST) + dot(
        cross_ref[days:, :], mine[:, half:], ((1,), (1,)), HIGHEST)
    for store in stores:
        store.wait()


def local(cells, grps, sketch, slab):
    k, days = sketch.shape[1], slab.shape[1]
    r_in, inverse, cross, held = factored(sketch, slab, cells, grps)
    vmem = pl.BlockSpec(memory_space=pltpu.VMEM)
    hbm = pl.BlockSpec(memory_space=pl.ANY)
    steps = len(chunks_of(sketch.shape[0], BASIS_STEP))
    r_factor, basis, projected = pl.pallas_call(
        basis_kernel,
        out_shape=(
            jax.ShapeDtypeStruct((k, k), jnp.float32),
            jax.ShapeDtypeStruct(sketch.shape, jnp.bfloat16),
            jax.ShapeDtypeStruct((days // grps, k // cells), jnp.float32),
        ),
        in_specs=[vmem] * 4,
        out_specs=(vmem, hbm, vmem),
        scratch_shapes=[
            pltpu.VMEM(sketch.shape, jnp.bfloat16),
            pltpu.SemaphoreType.DMA((steps,)),
        ],
        compiler_params=pltpu.CompilerParams(vmem_limit_bytes=VMEM_LIMIT),
        name="basis",
    )(r_in, inverse, cross, held)
    return r_factor, basis, projected.T


def solution(mesh):
    cells, grps = mesh.shape["cell"], mesh.shape["grp"]
    in_specs = (P(("parts", "cell", "grp"), None), P(("parts", "cell", "grp"), None))
    out_specs = (P("parts", None), P(("parts", "cell", "grp"), None), P(("parts", "cell"), "grp"))
    return jax.shard_map(
        functools.partial(local, cells, grps), mesh=mesh, in_specs=in_specs, out_specs=out_specs, check_vma=False)
```

```python
import functools

import jax
import jax.numpy as jnp
from jax import lax
from jax.experimental import pallas as pl
from jax.experimental.pallas import tpu as pltpu
from jax.sharding import PartitionSpec as P

SUB = 8
CORES = 2
VMEM_LIMIT = 20 * 2**20
SUM_STEP = 768
BASIS_STEP = 512
HIGHEST = lax.Precision.HIGHEST


def dot(a, b, contract, precision=None):
    return lax.dot_general(
        a, b, (contract, ((), ())), precision=precision, preferred_element_type=jnp.float32
    )


def chunks_of(total, step):
    return [pl.ds(start, min(step, total - start)) for start in range(0, total, step)]


def sums_over(a_ref, b_ref, loads):
    total = None
    for rows, load in loads:
        load.wait()
        part = dot(a_ref[rows, :], b_ref[rows, :], ((0,), (0,)))
        total = part if total is None else total + part
    return total


def tree(terms):
    while len(terms) > 1:
        terms = [a + b for a, b in zip(terms[::2], terms[1::2])]
    return terms[0]


def factor_base(block, ones_ref):
    n = block.shape[0]
    shape = (SUB, 2 * n)
    ones = ones_ref[:, : 2 * n]
    tiles = n // SUB
    sub = lax.broadcasted_iota(jnp.int32, shape, 0)
    lane = lax.broadcasted_iota(jnp.int32, shape, 1)
    eye = jnp.where(
        lax.broadcasted_iota(jnp.int32, (n, n), 0) == lax.broadcasted_iota(jnp.int32, (n, n), 1), 1.0, 0.0)
    wide = jnp.concatenate([block, eye.astype(jnp.float32)], axis=1)
    m = [wide[q * SUB : (q + 1) * SUB, :] for q in range(tiles)]
    done = []

    def row(x, j):
        return jnp.broadcast_to(x[j : j + 1, :], shape)

    def col(x, j):
        return jnp.broadcast_to(x[:, j : j + 1], shape)

    for p in range(tiles):
        t = m[p]
        c = [col(t, p * SUB + i) * ones for i in range(SUB)]
        s = {(j, i): row(c[i], j) for i in range(SUB) for j in range(i + 1)}
        r = jnp.zeros(shape, jnp.float32)
        for j in range(SUB):
            at = sub == j
            pivot = s[j, j]
            inv, root = 1.0 / pivot, lax.rsqrt(pivot)
            f = jnp.where(at, -inv, c[j] * inv)
            t_j = row(t, j)
            r = jnp.where(at, t_j * root, r)
            t = jnp.where(at, 0.0, t) - f * t_j
            scaled = {i: s[j, i] * inv for i in range(j + 1, SUB)}
            for i in range(j + 1, SUB):
                c[i] = jnp.where(at, 0.0, c[i]) - f * s[j, i]
                for h in range(j + 1, i + 1):
                    s[h, i] = s[h, i] - scaled[h] * s[j, i]
        done.append(jnp.where((lane >= sub + p * SUB), r, 0.0))
        if p + 1 < tiles:
            rows = [row(t, i) for i in range(SUB)]
            later = range(p + 1, tiles)
            terms = [[col(m[q], p * SUB + i) * rows[i] for q in later] for i in range(SUB)]
            for at, q in enumerate(later):
                m[q] = m[q] - tree([terms[i][at] for i in range(SUB)])
    done = jnp.concatenate(done, axis=0)
    return done[:, :n], done[:, n:]


def extend(r11, w11, g12, g22, ones_ref):
    h = r11.shape[0]
    r12 = dot(w11, g12, ((1,), (0,)), HIGHEST)
    r21 = r12.T
    r22, w22 = factor_base(g22 - dot(r21, r12, ((1,), (0,)), HIGHEST), ones_ref)
    w21 = -dot(w22, dot(r21, w11, ((1,), (0,)), HIGHEST), ((1,), (0,)), HIGHEST)
    zero = jnp.zeros((h, h), jnp.float32)
    return (
        jnp.concatenate([jnp.concatenate([r11, r12], axis=1), jnp.concatenate([zero, r22], axis=1)], axis=0),
        jnp.concatenate([jnp.concatenate([w11, zero], axis=1), jnp.concatenate([w21, w22], axis=1)], axis=0),
    )


def factor_kernel(
    cells, grps, sketch_hbm, slab_hbm, r_ref, inv_ref, cross_ref, sketch_ref,
    slab_ref, sketch_sems, slab_sems, ones_ref,
    own_a, core_a, chip_a, all_a, own_b, grp_b, cell_b, all_b,
    own_c, grp_c, cell_c, all_c, own_x, grp_x, cell_x,
    core_send, core_recv, a_send, a_recv, gb_send, gb_recv, zb_send, zb_recv, gc_send, gc_recv, zc_send, zc_recv,
    ac_send, ac_recv, gx_send, gx_recv, zx_send, zx_recv,
):
    def loading(source, target, sems):
        loads = []
        for i, rows in enumerate(chunks_of(source.shape[0], SUM_STEP)):
            load = pltpu.make_async_copy(source.at[rows, :], target.at[rows, :], sems.at[i])
            load.start()
            loads.append((rows, load))
        return loads

    sketch_loads = loading(sketch_hbm, sketch_ref, sketch_sems)
    slab_loads = loading(slab_hbm, slab_ref, slab_sems)
    me_c = lax.axis_index("cell")
    me_g = lax.axis_index("grp")
    chips_x = grps // CORES
    me_x, core = lax.div(me_g, CORES), lax.rem(me_g, CORES)
    me_chip = me_c * chips_x + me_x
    other = me_x * CORES + (1 - core)
    half = own_b.shape[1]
    quarter = half // 2
    started = []

    def send(source, target, send_sem, recv_sem, device):
        copy = pltpu.make_async_remote_copy(
            src_ref=source, dst_ref=target, send_sem=send_sem, recv_sem=recv_sem,
            device_id=device, device_id_type=pl.DeviceIdType.MESH)
        copy.start()
        started.append(copy)
        return copy

    def rows_of(ref, index, count):
        return ref.at[pl.ds(pl.multiple_of(index * count, SUB), count), :]

    grp_peers = [{"grp": lax.rem(me_g + d, grps)} for d in range(1, grps)]
    cell_peers = [{"cell": lax.rem(me_c + d, cells)} for d in range(1, cells)]
    chip_peers = [
        {"cell": lax.rem(me_c + dc, cells), "grp": lax.rem(me_x + dx, chips_x) * CORES + core}
        for dx in reversed(range(chips_x)) for dc in sorted(range(cells), key=lambda d: -min(d, cells - d)) if dc or dx]

    barrier = pltpu.get_barrier_semaphore()
    beyond = [{"cell": peer["cell"], "grp": peer["grp"]} for peer in chip_peers]
    for peer in beyond + [p for d, p in enumerate(grp_peers, 1)]:
        pl.semaphore_signal(barrier, inc=1, device_id=peer, device_id_type=pl.DeviceIdType.MESH)

    gram = sums_over(sketch_ref, sketch_ref, sketch_loads)
    eighth = quarter // 2
    own_a[...] = jnp.concatenate([gram[:eighth, :quarter], gram[eighth:quarter, :quarter]], axis=1)
    own_b[...] = jnp.concatenate([gram[:quarter, quarter:half], gram[quarter:half, quarter:half]], axis=1)
    pl.semaphore_wait(barrier, len(beyond) + len(grp_peers))

    def halves(own, landing, index):
        count = own.shape[0] // CORES
        return send(rows_of(own, 1 - core, count), landing, core_send.at[index], core_recv.at[index], {"grp": other})

    a1 = halves(own_a, core_a, 0)
    count = own_b.shape[0] // CORES
    b1 = [
        send(rows_of(own_b, lax.rem(peer["grp"], CORES), count), grp_b.at[me_g], gb_send.at[i], gb_recv.at[i], peer)
        for i, peer in enumerate(grp_peers)]
    own_c[0:half, :] = gram[:half, half:]
    own_c[half : half + quarter, :] = gram[half : half + quarter, half:]
    last = gram[half + quarter :, half + quarter :]
    own_c[half + quarter : half + quarter + eighth, :] = jnp.concatenate([last[:eighth], last[eighth:]], axis=1)
    spare = own_c.shape[0] - half - quarter - eighth
    if spare:
        own_c[half + quarter + eighth :, :] = jnp.zeros((spare, half), jnp.float32)

    def to_grps(own, landing, send_sems, recv_sems):
        count = own.shape[0] // grps
        return [
            send(rows_of(own, peer["grp"], count), landing.at[i], send_sems.at[i], recv_sems.at[i], peer)
            for i, peer in enumerate(grp_peers)]

    def sum_grps(copies, own, landing, slots):
        count = own.shape[0] // grps
        for copy in copies:
            copy.wait_recv()
        slots[me_c] = tree([own[pl.ds(pl.multiple_of(me_g * count, SUB), count), :]] + [landing[i] for i in range(grps - 1)])

    def spread(slots, me, peers, send_sems, recv_sems):
        return [send(slots.at[me], slots.at[me], send_sems.at[i], recv_sems.at[i], peer) for i, peer in enumerate(peers)]

    def sum_slots(copies, slots):
        for copy in copies:
            copy.wait_recv()
        return tree([slots[i] for i in range(slots.shape[0])])

    c1 = to_grps(own_c, grp_c, gc_send, gc_recv)

    def chip_sum(copy, own, landing, slots, send_sems, recv_sems):
        count = own.shape[0] // CORES
        copy.wait_recv()
        slots[me_chip] = own[pl.ds(pl.multiple_of(core * count, SUB), count), :] + landing[...]
        return spread(slots, me_chip, chip_peers, send_sems, recv_sems)

    a2 = chip_sum(a1, own_a, core_a, chip_a, a_send, a_recv)

    cross = sums_over(slab_ref, sketch_ref, slab_loads)
    days = cross.shape[0] // grps
    for g in range(grps):
        own_x[2 * g * days : (2 * g + 1) * days, :] = cross[g * days : (g + 1) * days, :half]
        own_x[(2 * g + 1) * days : 2 * (g + 1) * days, :] = cross[g * days : (g + 1) * days, half:]

    grp_b[me_g] = own_b[pl.ds(pl.multiple_of(core * (own_b.shape[0] // CORES), SUB), own_b.shape[0] // CORES), :]
    cell_b[me_c] = sum_slots(b1, grp_b)
    b2 = spread(cell_b, me_c, cell_peers, zb_send, zb_recv)
    sum_grps(c1, own_c, grp_c, cell_c)
    c2 = spread(cell_c, me_c, cell_peers, zc_send, zc_recv)

    def both(copies, slots, target, index):
        target[core] = sum_slots(copies, slots)
        return send(target.at[core], target.at[core], core_send.at[index], core_recv.at[index], {"grp": other})

    a3 = both(a2, chip_a, all_a, 2)
    ones_ref[...] = jnp.ones_like(ones_ref)
    b3 = both(b2, cell_b, all_b, 3)
    x1 = to_grps(own_x, grp_x, gx_send, gx_recv)

    a3.wait_recv()
    packed = jnp.concatenate([all_a[i] for i in range(CORES)], axis=0)
    first = jnp.concatenate([packed[:, :quarter], packed[:, quarter:]], axis=0)
    r_00, w_00 = factor_base(first, ones_ref)

    count = own_c.shape[0] // grps
    all_c[pl.ds(pl.multiple_of(me_g * count, SUB), count), :] = sum_slots(c2, cell_c)
    c3 = [
        send(rows_of(all_c, me_g, count), rows_of(all_c, me_g, count), ac_send.at[i], ac_recv.at[i], peer)
        for i, peer in enumerate(grp_peers)]

    b3.wait_recv()
    packed = jnp.concatenate([all_b[i] for i in range(CORES)], axis=0)
    r11, w11 = extend(r_00, w_00, packed[:, :quarter], packed[:, quarter:], ones_ref)
    zero = jnp.zeros((half, half), jnp.float32)
    r_ref[0:half, 0:half] = r11
    r_ref[half:, 0:half] = zero
    inv_ref[0:half, 0:half] = w11
    inv_ref[0:half, half:] = zero

    sum_grps(x1, own_x, grp_x, cell_x)
    x2 = spread(cell_x, me_c, cell_peers, zx_send, zx_recv)

    for copy in c3:
        copy.wait_recv()
    r12 = dot(w11, all_c[0:half, :], ((1,), (0,)), HIGHEST)
    r21 = r12.T
    taken = dot(r21, r12, ((1,), (0,)), HIGHEST)
    upper = all_c[half : half + quarter, :] - taken[:quarter]
    last = all_c[half + quarter : half + quarter + eighth, :]
    last = jnp.concatenate([last[:, :quarter], last[:, quarter:]], axis=0) - taken[quarter:, quarter:]
    mixed = dot(r21, w11, ((1,), (0,)), HIGHEST)
    r_ref[0:half, half:] = r12
    r_00, w_00 = factor_base(upper[:, :quarter], ones_ref)
    r22, w22 = extend(r_00, w_00, upper[:, quarter:], last, ones_ref)
    r_ref[half:, half:] = r22
    inv_ref[half:, 0:half] = -dot(w22, mixed, ((1,), (0,)), HIGHEST)
    inv_ref[half:, half:] = w22
    cross_ref[...] = sum_slots(x2, cell_x)
    for copy in started:
        copy.wait_send()


def factored(sketch, slab, cells, grps):
    k, days = sketch.shape[1], slab.shape[1]
    half, quarter = k // 2, k // 4
    chips = cells * grps // CORES
    f32 = jnp.float32
    dma = pltpu.SemaphoreType.DMA
    a_rows, b_rows, x_rows = quarter // 2, quarter, 2 * days
    c_rows = pl.cdiv(half + quarter + quarter // 2, SUB * grps) * SUB * grps
    assert grps % CORES == 0 and cells > 1 and k % (8 * SUB) == 0
    assert x_rows % (2 * SUB * grps) == 0

    def small(rows):
        part = rows // CORES
        return [pltpu.VMEM((rows, half), f32), pltpu.VMEM((part, half), f32),
                pltpu.VMEM((chips, part, half), f32), pltpu.VMEM((CORES, part, half), f32)]

    def large(rows):
        part = rows // grps
        return [pltpu.VMEM((rows, half), f32), pltpu.VMEM((grps - 1, part, half), f32),
                pltpu.VMEM((cells, part, half), f32)]

    return pl.pallas_call(
        functools.partial(factor_kernel, cells, grps),
        out_shape=(
            jax.ShapeDtypeStruct((k, k), f32),
            jax.ShapeDtypeStruct((k, k), f32),
            jax.ShapeDtypeStruct((x_rows // grps, half), f32),
            jax.ShapeDtypeStruct(sketch.shape, sketch.dtype),
        ),
        in_specs=[pl.BlockSpec(memory_space=pltpu.HBM)] * 2,
        out_specs=(pl.BlockSpec(memory_space=pltpu.VMEM),) * 4,
        scratch_shapes=[
            pltpu.VMEM(slab.shape, slab.dtype),
            dma((len(chunks_of(sketch.shape[0], SUM_STEP)),)),
            dma((len(chunks_of(slab.shape[0], SUM_STEP)),)),
            pltpu.VMEM((SUB, k), f32),
        ] + small(a_rows) + [
            pltpu.VMEM((b_rows, half), f32),
            pltpu.VMEM((grps, b_rows // CORES, half), f32),
            pltpu.VMEM((cells, b_rows // CORES, half), f32),
            pltpu.VMEM((CORES, b_rows // CORES, half), f32),
        ] + large(c_rows) + [pltpu.VMEM((c_rows, half), f32)] + large(x_rows)
        + [dma((4,))] * 2 + [dma((chips - 1,))] * 2 + [dma((grps - 1,))] * 2 + [dma((cells - 1,))] * 2
        + [dma((grps - 1,))] * 2 + [dma((cells - 1,))] * 2 + [dma((grps - 1,))] * 4 + [dma((cells - 1,))] * 2,
        compiler_params=pltpu.CompilerParams(collective_id=0, has_side_effects=True, vmem_limit_bytes=VMEM_LIMIT),
        name="reduce_and_factor",
    )(pltpu.with_memory_space_constraint(sketch, pltpu.HBM), pltpu.with_memory_space_constraint(slab, pltpu.HBM))


def basis_kernel(
    r_in, inv_ref, cross_ref, sketch_ref, r_out, basis_hbm, proj_ref, basis_ref, store_sems,
):
    steps = chunks_of(sketch_ref.shape[0], BASIS_STEP)
    half = cross_ref.shape[1]
    days = cross_ref.shape[0] // 2
    r_out[...] = r_in[...]
    whole = inv_ref[...]
    high = whole.astype(jnp.bfloat16)
    low = (whole - high.astype(jnp.float32)).astype(jnp.bfloat16)
    stores = []
    for i, rows in enumerate(steps):
        part = sketch_ref[rows, :]
        exact = dot(part, high, ((1,), (1,))) + dot(part, low, ((1,), (1,)))
        basis_ref[rows, :] = exact.astype(jnp.bfloat16)
        stores.append(pltpu.make_async_copy(basis_ref.at[rows, :], basis_hbm.at[rows, :], store_sems.at[i]))
        stores[-1].start()
    count = proj_ref.shape[1]
    mine = inv_ref[pl.ds(pl.multiple_of(lax.axis_index("cell") * count, SUB), count), :]
    proj_ref[...] = dot(cross_ref[0:days, :], mine[:, :half], ((1,), (1,)), HIGHEST) + dot(
        cross_ref[days:, :], mine[:, half:], ((1,), (1,)), HIGHEST)
    for store in stores:
        store.wait()


def local(cells, grps, sketch, slab):
    k, days = sketch.shape[1], slab.shape[1]
    r_in, inverse, cross, held = factored(sketch, slab, cells, grps)
    vmem = pl.BlockSpec(memory_space=pltpu.VMEM)
    hbm = pl.BlockSpec(memory_space=pl.ANY)
    steps = len(chunks_of(sketch.shape[0], BASIS_STEP))
    r_factor, basis, projected = pl.pallas_call(
        basis_kernel,
        out_shape=(
            jax.ShapeDtypeStruct((k, k), jnp.float32),
            jax.ShapeDtypeStruct(sketch.shape, jnp.bfloat16),
            jax.ShapeDtypeStruct((days // grps, k // cells), jnp.float32),
        ),
        in_specs=[vmem] * 4,
        out_specs=(vmem, hbm, vmem),
        scratch_shapes=[
            pltpu.VMEM(sketch.shape, jnp.bfloat16),
            pltpu.SemaphoreType.DMA((steps,)),
        ],
        compiler_params=pltpu.CompilerParams(vmem_limit_bytes=VMEM_LIMIT),
        name="basis",
    )(r_in, inverse, cross, held)
    return r_factor, basis, projected.T


def solution(mesh):
    cells, grps = mesh.shape["cell"], mesh.shape["grp"]
    in_specs = (P(("parts", "cell", "grp"), None), P(("parts", "cell", "grp"), None))
    out_specs = (P("parts", None), P(("parts", "cell", "grp"), None), P(("parts", "cell"), "grp"))
    return jax.shard_map(
        functools.partial(local, cells, grps), mesh=mesh, in_specs=in_specs, out_specs=out_specs, check_vma=False)
```

```python
import functools

import jax
import jax.numpy as jnp
from jax import lax
from jax.experimental import pallas as pl
from jax.experimental.pallas import tpu as pltpu
from jax.sharding import PartitionSpec as P

SUB = 8
CORES = 2
VMEM_LIMIT = 20 * 2**20
SUM_STEP = 768
BASIS_STEP = 512
HIGHEST = lax.Precision.HIGHEST


def dot(a, b, contract, precision=None):
    return lax.dot_general(
        a, b, (contract, ((), ())), precision=precision, preferred_element_type=jnp.float32
    )


def chunks_of(total, step):
    return [pl.ds(start, min(step, total - start)) for start in range(0, total, step)]


def sums_over(a_ref, b_ref, loads):
    total = None
    for rows, load in loads:
        load.wait()
        part = dot(a_ref[rows, :], b_ref[rows, :], ((0,), (0,)))
        total = part if total is None else total + part
    return total


def tree(terms):
    terms=list(terms)
    while len(terms) > 1:
        terms = [a + b for a, b in zip(terms[::2], terms[1::2])] + terms[len(terms) // 2 * 2 :]
    return terms[0]

def factor_base(block, ones_ref):
    n = block.shape[0]
    shape = (SUB, 2 * n)
    ones = ones_ref[:, : 2 * n]
    tiles = n // SUB
    sub = lax.broadcasted_iota(jnp.int32, shape, 0)
    lane = lax.broadcasted_iota(jnp.int32, shape, 1)
    eye = jnp.where(
        lax.broadcasted_iota(jnp.int32, (n, n), 0) == lax.broadcasted_iota(jnp.int32, (n, n), 1), 1.0, 0.0)
    wide = jnp.concatenate([block, eye.astype(jnp.float32)], axis=1)
    m = [wide[q * SUB : (q + 1) * SUB, :] for q in range(tiles)]
    done = []

    def row(x, j):
        return jnp.broadcast_to(x[j : j + 1, :], shape)

    def col(x, j):
        return jnp.broadcast_to(x[:, j : j + 1], shape)

    for p in range(tiles):
        t = m[p]
        c = [col(t, p * SUB + i) * ones for i in range(SUB)]
        corner = [row(c[0], 0), row(c[1], 0), row(c[1], 1)]
        r = jnp.zeros(shape, jnp.float32)
        for j in range(0, SUB, 2):
            k = j + 1
            at_j, at_k = sub == j, sub == k
            pair = at_j | at_k
            a, b, d = corner
            det = a * d - b * b
            inv = 1.0 / det
            root_a, root = lax.rsqrt(a), lax.rsqrt(det)
            f_j = jnp.where(at_j, -d, jnp.where(at_k, b, c[j] * d - c[k] * b))
            f_k = jnp.where(at_j, b, jnp.where(at_k, -a, c[k] * a - c[j] * b))
            t_j, t_k = row(t, j), row(t, k)
            r = jnp.where(at_j, t_j * root_a, jnp.where(at_k, (t_k * a - t_j * b) * (root_a * root), r))
            t = jnp.where(pair, 0.0, t) - (f_j * t_j + f_k * t_k) * inv
            if k + 1 < SUB:
                s_j = {i: row(c[i], j) for i in range(k + 1, SUB)}
                s_k = {i: row(c[i], k) for i in range(k + 1, SUB)}
                e, g = k + 1, k + 2
                v = {h: (s_j[h] * d - s_k[h] * b, s_k[h] * a - s_j[h] * b) for h in (e, g)}
                corner = [
                    row(c[i], h) - (v[h][0] * s_j[i] + v[h][1] * s_k[i]) * inv for h, i in ((e, e), (e, g), (g, g))]
                for i in range(k + 1, SUB):
                    c[i] = jnp.where(pair, 0.0, c[i]) - (f_j * s_j[i] + f_k * s_k[i]) * inv
        done.append(jnp.where((lane >= sub + p * SUB), r, 0.0))
        if p + 1 < tiles:
            rows = [row(t, i) for i in range(SUB)]
            later = range(p + 1, tiles)
            terms = [[col(m[q], p * SUB + i) * rows[i] for q in later] for i in range(SUB)]
            for at, q in enumerate(later):
                m[q] = m[q] - tree([terms[i][at] for i in range(SUB)])
    done = jnp.concatenate(done, axis=0)
    return done[:, :n], done[:, n:]


def scales(block):
    n = block.shape[0]
    eye = lax.broadcasted_iota(jnp.int32, (n, n), 0) == lax.broadcasted_iota(jnp.int32, (n, n), 1)
    kept = jnp.where(eye, block, 0.0)
    across = jnp.sum(kept, axis=0, keepdims=True)
    row, col = lax.rsqrt(across), lax.rsqrt(jnp.sum(kept, axis=1, keepdims=True))
    return row, col, across * row


def extend(r11, w11, g12, g22, ones_ref):
    h = r11.shape[0]
    r12 = dot(w11, g12, ((1,), (0,)), HIGHEST)
    r21 = r12.T
    r22, w22 = factor_base(g22 - dot(r21, r12, ((1,), (0,)), HIGHEST), ones_ref)
    w21 = -dot(w22, dot(r21, w11, ((1,), (0,)), HIGHEST), ((1,), (0,)), HIGHEST)
    zero = jnp.zeros((h, h), jnp.float32)
    return (
        jnp.concatenate([jnp.concatenate([r11, r12], axis=1), jnp.concatenate([zero, r22], axis=1)], axis=0),
        jnp.concatenate([jnp.concatenate([w11, zero], axis=1), jnp.concatenate([w21, w22], axis=1)], axis=0),
    )


def factor_kernel(
    cells, grps, sketch_hbm, slab_hbm, r_ref, inv_ref, cross_ref, sketch_ref,
    slab_ref, sketch_sems, slab_sems, ones_ref,
    own_a, core_a, chip_a, all_a, own_b, grp_b, cell_b, all_b,
    own_c, grp_c, cell_c, all_c, own_x, grp_x, cell_x,
    core_send, core_recv, a_send, a_recv, gb_send, gb_recv, zb_send, zb_recv, gc_send, gc_recv, zc_send, zc_recv,
    ac_send, ac_recv, gx_send, gx_recv, zx_send, zx_recv,
):
    def loading(source, target, sems):
        loads = []
        for i, rows in enumerate(chunks_of(source.shape[0], SUM_STEP)):
            load = pltpu.make_async_copy(source.at[rows, :], target.at[rows, :], sems.at[i])
            load.start()
            loads.append((rows, load))
        return loads

    sketch_loads = loading(sketch_hbm, sketch_ref, sketch_sems)
    slab_loads = loading(slab_hbm, slab_ref, slab_sems)
    me_c = lax.axis_index("cell")
    me_g = lax.axis_index("grp")
    chips_x = grps // CORES
    me_x, core = lax.div(me_g, CORES), lax.rem(me_g, CORES)
    me_chip = me_c * chips_x + me_x
    other = me_x * CORES + (1 - core)
    half = own_b.shape[1]
    quarter = half // 2
    started = []

    def send(source, target, send_sem, recv_sem, device):
        copy = pltpu.make_async_remote_copy(
            src_ref=source, dst_ref=target, send_sem=send_sem, recv_sem=recv_sem,
            device_id=device, device_id_type=pl.DeviceIdType.MESH)
        copy.start()
        started.append(copy)
        return copy

    def rows_of(ref, index, count):
        return ref.at[pl.ds(pl.multiple_of(index * count, SUB), count), :]

    grp_peers = [{"grp": lax.rem(me_g + d, grps)} for d in range(1, grps)]
    cell_peers = [{"cell": lax.rem(me_c + d, cells)} for d in range(1, cells)]
    chip_peers = [
        {"cell": lax.rem(me_c + dc, cells), "grp": lax.rem(me_x + dx, chips_x) * CORES + core}
        for dx in reversed(range(chips_x)) for dc in sorted(range(cells), key=lambda d: -min(d, cells - d)) if dc or dx]

    barrier = pltpu.get_barrier_semaphore()
    beyond = [{"cell": peer["cell"], "grp": peer["grp"]} for peer in chip_peers]
    for peer in beyond + [p for d, p in enumerate(grp_peers, 1)]:
        pl.semaphore_signal(barrier, inc=1, device_id=peer, device_id_type=pl.DeviceIdType.MESH)

    gram = sums_over(sketch_ref, sketch_ref, sketch_loads)
    eighth = quarter // 2
    own_a[...] = jnp.concatenate([gram[:eighth, :quarter], gram[eighth:quarter, :quarter]], axis=1)
    own_b[...] = jnp.concatenate([gram[:quarter, quarter:half], gram[quarter:half, quarter:half]], axis=1)
    pl.semaphore_wait(barrier, len(beyond) + len(grp_peers))

    def halves(own, landing, index):
        count = own.shape[0] // CORES
        return send(rows_of(own, 1 - core, count), landing, core_send.at[index], core_recv.at[index], {"grp": other})

    a1 = halves(own_a, core_a, 0)
    count = own_b.shape[0] // CORES
    b1 = [
        send(rows_of(own_b, lax.rem(peer["grp"], CORES), count), grp_b.at[me_g], gb_send.at[i], gb_recv.at[i], peer)
        for i, peer in enumerate(grp_peers)]
    own_c[0:half, :] = gram[:half, half:]
    own_c[half : half + quarter, :] = gram[half : half + quarter, half:]
    last = gram[half + quarter :, half + quarter :]
    own_c[half + quarter : half + quarter + eighth, :] = jnp.concatenate([last[:eighth], last[eighth:]], axis=1)
    spare = own_c.shape[0] - half - quarter - eighth
    if spare:
        own_c[half + quarter + eighth :, :] = jnp.zeros((spare, half), jnp.float32)

    def to_grps(own, landing, send_sems, recv_sems):
        count = own.shape[0] // grps
        return [
            send(rows_of(own, peer["grp"], count), landing.at[i], send_sems.at[i], recv_sems.at[i], peer)
            for i, peer in enumerate(grp_peers)]

    def sum_grps(copies, own, landing, slots):
        count = own.shape[0] // grps
        for copy in copies:
            copy.wait_recv()
        slots[me_c] = tree([own[pl.ds(pl.multiple_of(me_g * count, SUB), count), :]] + [landing[i] for i in range(grps - 1)])

    def spread(slots, me, peers, send_sems, recv_sems):
        return [send(slots.at[me], slots.at[me], send_sems.at[i], recv_sems.at[i], peer) for i, peer in enumerate(peers)]

    def sum_slots(copies, slots):
        for copy in copies:
            copy.wait_recv()
        return tree([slots[i] for i in range(slots.shape[0])])

    c1 = to_grps(own_c, grp_c, gc_send, gc_recv)

    def chip_sum(copy, own, landing, slots, send_sems, recv_sems):
        count = own.shape[0] // CORES
        copy.wait_recv()
        slots[me_chip] = own[pl.ds(pl.multiple_of(core * count, SUB), count), :] + landing[...]
        return spread(slots, me_chip, chip_peers, send_sems, recv_sems)

    a2 = chip_sum(a1, own_a, core_a, chip_a, a_send, a_recv)

    cross = sums_over(slab_ref, sketch_ref, slab_loads)
    days = cross.shape[0] // grps
    for g in range(grps):
        own_x[2 * g * days : (2 * g + 1) * days, :] = cross[g * days : (g + 1) * days, :half]
        own_x[(2 * g + 1) * days : 2 * (g + 1) * days, :] = cross[g * days : (g + 1) * days, half:]

    grp_b[me_g] = own_b[pl.ds(pl.multiple_of(core * (own_b.shape[0] // CORES), SUB), own_b.shape[0] // CORES), :]
    cell_b[me_c] = sum_slots(b1, grp_b)
    b2 = spread(cell_b, me_c, cell_peers, zb_send, zb_recv)
    sum_grps(c1, own_c, grp_c, cell_c)
    c2 = spread(cell_c, me_c, cell_peers, zc_send, zc_recv)

    def both(copies, slots, target, index):
        target[core] = sum_slots(copies, slots)
        return send(target.at[core], target.at[core], core_send.at[index], core_recv.at[index], {"grp": other})

    a3 = both(a2, chip_a, all_a, 2)
    ones_ref[...] = jnp.ones_like(ones_ref)
    b3 = both(b2, cell_b, all_b, 3)
    x1 = to_grps(own_x, grp_x, gx_send, gx_recv)

    a3.wait_recv()
    packed = jnp.concatenate([all_a[i] for i in range(CORES)], axis=0)
    first = jnp.concatenate([packed[:, :quarter], packed[:, quarter:]], axis=0)
    row0, col0, back0 = scales(first)
    r_00, w_00 = factor_base(first * col0 * row0, ones_ref)

    count = own_c.shape[0] // grps
    all_c[pl.ds(pl.multiple_of(me_g * count, SUB), count), :] = sum_slots(c2, cell_c)
    c3 = [
        send(rows_of(all_c, me_g, count), rows_of(all_c, me_g, count), ac_send.at[i], ac_recv.at[i], peer)
        for i, peer in enumerate(grp_peers)]

    b3.wait_recv()
    packed = jnp.concatenate([all_b[i] for i in range(CORES)], axis=0)
    row1, col1, back1 = scales(packed[:, quarter:])
    r11, w11 = extend(
        r_00, w_00, packed[:, :quarter] * col0 * row1, packed[:, quarter:] * col1 * row1, ones_ref)
    left_row, left_col = jnp.concatenate([row0, row1], axis=1), jnp.concatenate([col0, col1], axis=0)
    zero = jnp.zeros((half, half), jnp.float32)
    r_ref[0:half, 0:half] = r11 * jnp.concatenate([back0, back1], axis=1)
    r_ref[half:, 0:half] = zero
    inv_ref[0:half, 0:half] = w11 * left_row
    inv_ref[0:half, half:] = zero

    sum_grps(x1, own_x, grp_x, cell_x)
    x2 = spread(cell_x, me_c, cell_peers, zx_send, zx_recv)

    for copy in c3:
        copy.wait_recv()
    upper = all_c[half : half + quarter, :]
    last = all_c[half + quarter : half + quarter + eighth, :]
    last = jnp.concatenate([last[:, :quarter], last[:, quarter:]], axis=0)
    row2, col2, back2 = scales(upper[:, :quarter])
    row3, col3, back3 = scales(last)
    right_row, back = jnp.concatenate([row2, row3], axis=1), jnp.concatenate([back2, back3], axis=1)
    r12 = dot(w11, all_c[0:half, :] * left_col * right_row, ((1,), (0,)), HIGHEST)
    r21 = r12.T
    taken = dot(r21, r12, ((1,), (0,)), HIGHEST)
    upper = upper * col2 * right_row - taken[:quarter]
    last = last * col3 * row3 - taken[quarter:, quarter:]
    mixed = dot(r21, w11, ((1,), (0,)), HIGHEST)
    r_ref[0:half, half:] = r12 * back
    r_00, w_00 = factor_base(upper[:, :quarter], ones_ref)
    r22, w22 = extend(r_00, w_00, upper[:, quarter:], last, ones_ref)
    r_ref[half:, half:] = r22 * back
    inv_ref[half:, 0:half] = -dot(w22, mixed, ((1,), (0,)), HIGHEST) * left_row
    inv_ref[half:, half:] = w22 * right_row
    cross_ref[...] = sum_slots(x2, cell_x)
    for copy in started:
        copy.wait_send()


def factored(sketch, slab, cells, grps):
    k, days = sketch.shape[1], slab.shape[1]
    half, quarter = k // 2, k // 4
    chips = cells * grps // CORES
    f32 = jnp.float32
    dma = pltpu.SemaphoreType.DMA
    a_rows, b_rows, x_rows = quarter // 2, quarter, 2 * days
    c_rows = pl.cdiv(half + quarter + quarter // 2, SUB * grps) * SUB * grps
    assert grps % CORES == 0 and cells > 1 and k % (8 * SUB) == 0
    assert x_rows % (2 * SUB * grps) == 0

    def small(rows):
        part = rows // CORES
        return [pltpu.VMEM((rows, half), f32), pltpu.VMEM((part, half), f32),
                pltpu.VMEM((chips, part, half), f32), pltpu.VMEM((CORES, part, half), f32)]

    def large(rows):
        part = rows // grps
        return [pltpu.VMEM((rows, half), f32), pltpu.VMEM((grps - 1, part, half), f32),
                pltpu.VMEM((cells, part, half), f32)]

    return pl.pallas_call(
        functools.partial(factor_kernel, cells, grps),
        out_shape=(
            jax.ShapeDtypeStruct((k, k), f32),
            jax.ShapeDtypeStruct((k, k), f32),
            jax.ShapeDtypeStruct((x_rows // grps, half), f32),
            jax.ShapeDtypeStruct(sketch.shape, sketch.dtype),
        ),
        in_specs=[pl.BlockSpec(memory_space=pltpu.HBM)] * 2,
        out_specs=(pl.BlockSpec(memory_space=pltpu.VMEM),) * 4,
        scratch_shapes=[
            pltpu.VMEM(slab.shape, slab.dtype),
            dma((len(chunks_of(sketch.shape[0], SUM_STEP)),)),
            dma((len(chunks_of(slab.shape[0], SUM_STEP)),)),
            pltpu.VMEM((SUB, k), f32),
        ] + small(a_rows) + [
            pltpu.VMEM((b_rows, half), f32),
            pltpu.VMEM((grps, b_rows // CORES, half), f32),
            pltpu.VMEM((cells, b_rows // CORES, half), f32),
            pltpu.VMEM((CORES, b_rows // CORES, half), f32),
        ] + large(c_rows) + [pltpu.VMEM((c_rows, half), f32)] + large(x_rows)
        + [dma((4,))] * 2 + [dma((chips - 1,))] * 2 + [dma((grps - 1,))] * 2 + [dma((cells - 1,))] * 2
        + [dma((grps - 1,))] * 2 + [dma((cells - 1,))] * 2 + [dma((grps - 1,))] * 4 + [dma((cells - 1,))] * 2,
        compiler_params=pltpu.CompilerParams(collective_id=0, has_side_effects=True, vmem_limit_bytes=VMEM_LIMIT),
        name="reduce_and_factor",
    )(pltpu.with_memory_space_constraint(sketch, pltpu.HBM), pltpu.with_memory_space_constraint(slab, pltpu.HBM))


def basis_kernel(
    r_in, inv_ref, cross_ref, sketch_ref, r_hbm, basis_hbm, proj_ref, basis_ref, r_sem, store_sems,
):
    steps = chunks_of(sketch_ref.shape[0], BASIS_STEP)
    half = cross_ref.shape[1]
    days = cross_ref.shape[0] // 2
    stores = [pltpu.make_async_copy(r_in, r_hbm, r_sem)]
    stores[0].start()
    whole = inv_ref[...]
    high = whole.astype(jnp.bfloat16)
    low = (whole - high.astype(jnp.float32)).astype(jnp.bfloat16)
    for i, rows in enumerate(steps):
        part = sketch_ref[rows, :]
        exact = dot(part, high, ((1,), (1,))) + dot(part, low, ((1,), (1,)))
        basis_ref[rows, :] = exact.astype(jnp.bfloat16)
        stores.append(pltpu.make_async_copy(basis_ref.at[rows, :], basis_hbm.at[rows, :], store_sems.at[i]))
        stores[-1].start()
    count = proj_ref.shape[1]
    mine = inv_ref[pl.ds(pl.multiple_of(lax.axis_index("cell") * count, SUB), count), :]
    proj_ref[...] = dot(cross_ref[0:days, :], mine[:, :half], ((1,), (1,)), HIGHEST) + dot(
        cross_ref[days:, :], mine[:, half:], ((1,), (1,)), HIGHEST)
    for store in stores:
        store.wait()


def local(cells, grps, sketch, slab):
    k, days = sketch.shape[1], slab.shape[1]
    r_in, inverse, cross, held = factored(sketch, slab, cells, grps)
    vmem = pl.BlockSpec(memory_space=pltpu.VMEM)
    hbm = pl.BlockSpec(memory_space=pl.ANY)
    steps = len(chunks_of(sketch.shape[0], BASIS_STEP))
    r_factor, basis, projected = pl.pallas_call(
        basis_kernel,
        out_shape=(
            jax.ShapeDtypeStruct((k, k), jnp.float32),
            jax.ShapeDtypeStruct(sketch.shape, jnp.bfloat16),
            jax.ShapeDtypeStruct((days // grps, k // cells), jnp.float32),
        ),
        in_specs=[vmem] * 4,
        out_specs=(hbm, hbm, vmem),
        scratch_shapes=[
            pltpu.VMEM(sketch.shape, jnp.bfloat16),
            pltpu.SemaphoreType.DMA,
            pltpu.SemaphoreType.DMA((steps,)),
        ],
        compiler_params=pltpu.CompilerParams(vmem_limit_bytes=VMEM_LIMIT),
        name="basis",
    )(r_in, inverse, cross, held)
    return r_factor, basis, projected.T


def solution(mesh):
    cells, grps = mesh.shape["cell"], mesh.shape["grp"]
    in_specs = (P(("parts", "cell", "grp"), None), P(("parts", "cell", "grp"), None))
    out_specs = (P("parts", None), P(("parts", "cell", "grp"), None), P(("parts", "cell"), "grp"))
    return jax.shard_map(
        functools.partial(local, cells, grps), mesh=mesh, in_specs=in_specs, out_specs=out_specs, check_vma=False)
```

```python
import functools

import jax
import jax.numpy as jnp
from jax import lax
from jax.experimental import pallas as pl
from jax.experimental.pallas import tpu as pltpu
from jax.sharding import PartitionSpec as P

SUB = 8
CORES = 2
VMEM_LIMIT = 20 * 2**20
SUM_STEP = 768
BASIS_STEP = 512
HIGHEST = lax.Precision.HIGHEST


def dot(a, b, contract, precision=None):
    return lax.dot_general(
        a, b, (contract, ((), ())), precision=precision, preferred_element_type=jnp.float32
    )


def chunks_of(total, step):
    return [pl.ds(start, min(step, total - start)) for start in range(0, total, step)]


def sums_over(a_ref, b_ref, loads):
    total = None
    for rows, load in loads:
        load.wait()
        part = dot(a_ref[rows, :], b_ref[rows, :], ((0,), (0,)))
        total = part if total is None else total + part
    return total


def tree(terms):
    terms=list(terms)
    while len(terms) > 1:
        terms = [a + b for a, b in zip(terms[::2], terms[1::2])] + terms[len(terms) // 2 * 2 :]
    return terms[0]

def factor_base(block, ones_ref):
    n = block.shape[0]
    shape = (SUB, 2 * n)
    ones = ones_ref[:, : 2 * n]
    tiles = n // SUB
    sub = lax.broadcasted_iota(jnp.int32, shape, 0)
    lane = lax.broadcasted_iota(jnp.int32, shape, 1)
    eye = jnp.where(
        lax.broadcasted_iota(jnp.int32, (n, n), 0) == lax.broadcasted_iota(jnp.int32, (n, n), 1), 1.0, 0.0)
    wide = jnp.concatenate([block, eye.astype(jnp.float32)], axis=1)
    m = [wide[q * SUB : (q + 1) * SUB, :] for q in range(tiles)]
    done = []
    ahead = None

    def row(x, j):
        return jnp.broadcast_to(x[j : j + 1, :], shape)

    def col(x, j):
        return jnp.broadcast_to(x[:, j : j + 1], shape)

    for p in range(tiles):
        t = m[p]
        c = [col(t, p * SUB + i) * ones for i in range(0 if ahead is None else 2, SUB)]
        c = c if ahead is None else ahead + c
        after = m[p + 1] if p + 1 < tiles else None
        if after is not None:
            e = [col(after, p * SUB + i) * ones for i in range(SUB)]
            ahead = [col(after, (p + 1) * SUB + i) * ones for i in range(2)]
        corner = [row(c[0], 0), row(c[1], 0), row(c[1], 1)]
        r = jnp.zeros(shape, jnp.float32)
        for j in range(0, SUB, 2):
            k = j + 1
            at_j, at_k = sub == j, sub == k
            pair = at_j | at_k
            a, b, d = corner
            det = a * d - b * b
            inv = 1.0 / det
            root_a, root = lax.rsqrt(a), lax.rsqrt(det)
            f_j = jnp.where(at_j, -d, jnp.where(at_k, b, c[j] * d - c[k] * b))
            f_k = jnp.where(at_j, b, jnp.where(at_k, -a, c[k] * a - c[j] * b))
            t_j, t_k = row(t, j), row(t, k)
            r = jnp.where(at_j, t_j * root_a, jnp.where(at_k, (t_k * a - t_j * b) * (root_a * root), r))
            t = jnp.where(pair, 0.0, t) - (f_j * t_j + f_k * t_k) * inv
            if after is not None:
                n_j, n_k = e[j] * d - e[k] * b, e[k] * a - e[j] * b
                ahead = [x - (n_j * row(e[j], i) + n_k * row(e[k], i)) * inv for i, x in enumerate(ahead)]
            if k + 1 < SUB:
                s_j = {i: row(c[i], j) for i in range(k + 1, SUB)}
                s_k = {i: row(c[i], k) for i in range(k + 1, SUB)}
                x, y = k + 1, k + 2
                v = {h: (s_j[h] * d - s_k[h] * b, s_k[h] * a - s_j[h] * b) for h in (x, y)}
                corner = [
                    row(c[i], h) - (v[h][0] * s_j[i] + v[h][1] * s_k[i]) * inv for h, i in ((x, x), (x, y), (y, y))]
                for i in range(k + 1, SUB):
                    c[i] = jnp.where(pair, 0.0, c[i]) - (f_j * s_j[i] + f_k * s_k[i]) * inv
                    if after is not None:
                        e[i] = e[i] - (n_j * s_j[i] + n_k * s_k[i]) * inv
        done.append(jnp.where((lane >= sub + p * SUB), r, 0.0))
        if p + 1 < tiles:
            rows = [row(t, i) for i in range(SUB)]
            later = range(p + 1, tiles)
            terms = [[col(m[q], p * SUB + i) * rows[i] for q in later] for i in range(SUB)]
            for at, q in enumerate(later):
                m[q] = m[q] - tree([terms[i][at] for i in range(SUB)])
    done = jnp.concatenate(done, axis=0)
    return done[:, :n], done[:, n:]


def scales(block):
    n = block.shape[0]
    eye = lax.broadcasted_iota(jnp.int32, (n, n), 0) == lax.broadcasted_iota(jnp.int32, (n, n), 1)
    kept = jnp.where(eye, block, 0.0)
    across = jnp.sum(kept, axis=0, keepdims=True)
    row, col = lax.rsqrt(across), lax.rsqrt(jnp.sum(kept, axis=1, keepdims=True))
    return row, col, across * row


def extend(r11, w11, g12, g22, ones_ref):
    h = r11.shape[0]
    r12 = dot(w11, g12, ((1,), (0,)), HIGHEST)
    r21 = r12.T
    r22, w22 = factor_base(g22 - dot(r21, r12, ((1,), (0,)), HIGHEST), ones_ref)
    w21 = -dot(w22, dot(r21, w11, ((1,), (0,)), HIGHEST), ((1,), (0,)), HIGHEST)
    zero = jnp.zeros((h, h), jnp.float32)
    return (
        jnp.concatenate([jnp.concatenate([r11, r12], axis=1), jnp.concatenate([zero, r22], axis=1)], axis=0),
        jnp.concatenate([jnp.concatenate([w11, zero], axis=1), jnp.concatenate([w21, w22], axis=1)], axis=0),
    )


def factor_kernel(
    cells, grps, sketch_hbm, slab_hbm, r_ref, inv_ref, cross_ref, sketch_ref,
    slab_ref, sketch_sems, slab_sems, ones_ref,
    own_a, core_a, chip_a, all_a, own_b, grp_b, cell_b, all_b,
    own_c, grp_c, cell_c, all_c, own_x, grp_x, cell_x,
    core_send, core_recv, a_send, a_recv, gb_send, gb_recv, zb_send, zb_recv, gc_send, gc_recv, zc_send, zc_recv,
    ac_send, ac_recv, gx_send, gx_recv, zx_send, zx_recv,
):
    def loading(source, target, sems):
        loads = []
        for i, rows in enumerate(chunks_of(source.shape[0], SUM_STEP)):
            load = pltpu.make_async_copy(source.at[rows, :], target.at[rows, :], sems.at[i])
            load.start()
            loads.append((rows, load))
        return loads

    sketch_loads = loading(sketch_hbm, sketch_ref, sketch_sems)
    slab_loads = loading(slab_hbm, slab_ref, slab_sems)
    me_c = lax.axis_index("cell")
    me_g = lax.axis_index("grp")
    chips_x = grps // CORES
    me_x, core = lax.div(me_g, CORES), lax.rem(me_g, CORES)
    me_chip = me_c * chips_x + me_x
    other = me_x * CORES + (1 - core)
    half = own_b.shape[1]
    quarter = half // 2
    started = []

    def send(source, target, send_sem, recv_sem, device):
        copy = pltpu.make_async_remote_copy(
            src_ref=source, dst_ref=target, send_sem=send_sem, recv_sem=recv_sem,
            device_id=device, device_id_type=pl.DeviceIdType.MESH)
        copy.start()
        started.append(copy)
        return copy

    def rows_of(ref, index, count):
        return ref.at[pl.ds(pl.multiple_of(index * count, SUB), count), :]

    grp_peers = [{"grp": lax.rem(me_g + d, grps)} for d in range(1, grps)]
    cell_peers = [{"cell": lax.rem(me_c + d, cells)} for d in range(1, cells)]
    chip_peers = [
        {"cell": lax.rem(me_c + dc, cells), "grp": lax.rem(me_x + dx, chips_x) * CORES + core}
        for dx in reversed(range(chips_x)) for dc in sorted(range(cells), key=lambda d: -min(d, cells - d)) if dc or dx]

    barrier = pltpu.get_barrier_semaphore()
    beyond = [{"cell": peer["cell"], "grp": peer["grp"]} for peer in chip_peers]
    for peer in beyond + [p for d, p in enumerate(grp_peers, 1)]:
        pl.semaphore_signal(barrier, inc=1, device_id=peer, device_id_type=pl.DeviceIdType.MESH)

    gram = sums_over(sketch_ref, sketch_ref, sketch_loads)
    eighth = quarter // 2
    own_a[...] = jnp.concatenate([gram[:eighth, :quarter], gram[eighth:quarter, :quarter]], axis=1)
    own_b[...] = jnp.concatenate([gram[:quarter, quarter:half], gram[quarter:half, quarter:half]], axis=1)
    pl.semaphore_wait(barrier, len(beyond) + len(grp_peers))

    def halves(own, landing, index):
        count = own.shape[0] // CORES
        return send(rows_of(own, 1 - core, count), landing, core_send.at[index], core_recv.at[index], {"grp": other})

    a1 = halves(own_a, core_a, 0)
    count = own_b.shape[0] // CORES
    b1 = [
        send(rows_of(own_b, lax.rem(peer["grp"], CORES), count), grp_b.at[me_g], gb_send.at[i], gb_recv.at[i], peer)
        for i, peer in enumerate(grp_peers)]
    own_c[0:half, :] = gram[:half, half:]
    own_c[half : half + quarter, :] = gram[half : half + quarter, half:]
    last = gram[half + quarter :, half + quarter :]
    own_c[half + quarter : half + quarter + eighth, :] = jnp.concatenate([last[:eighth], last[eighth:]], axis=1)
    spare = own_c.shape[0] - half - quarter - eighth
    if spare:
        own_c[half + quarter + eighth :, :] = jnp.zeros((spare, half), jnp.float32)

    def to_grps(own, landing, send_sems, recv_sems):
        count = own.shape[0] // grps
        return [
            send(rows_of(own, peer["grp"], count), landing.at[i], send_sems.at[i], recv_sems.at[i], peer)
            for i, peer in enumerate(grp_peers)]

    def sum_grps(copies, own, landing, slots):
        count = own.shape[0] // grps
        for copy in copies:
            copy.wait_recv()
        slots[me_c] = tree([own[pl.ds(pl.multiple_of(me_g * count, SUB), count), :]] + [landing[i] for i in range(grps - 1)])

    def spread(slots, me, peers, send_sems, recv_sems):
        return [send(slots.at[me], slots.at[me], send_sems.at[i], recv_sems.at[i], peer) for i, peer in enumerate(peers)]

    def sum_slots(copies, slots):
        for copy in copies:
            copy.wait_recv()
        return tree([slots[i] for i in range(slots.shape[0])])

    c1 = to_grps(own_c, grp_c, gc_send, gc_recv)

    def chip_sum(copy, own, landing, slots, send_sems, recv_sems):
        count = own.shape[0] // CORES
        copy.wait_recv()
        slots[me_chip] = own[pl.ds(pl.multiple_of(core * count, SUB), count), :] + landing[...]
        return spread(slots, me_chip, chip_peers, send_sems, recv_sems)

    a2 = chip_sum(a1, own_a, core_a, chip_a, a_send, a_recv)

    cross = sums_over(slab_ref, sketch_ref, slab_loads)
    days = cross.shape[0] // grps
    for g in range(grps):
        own_x[2 * g * days : (2 * g + 1) * days, :] = cross[g * days : (g + 1) * days, :half]
        own_x[(2 * g + 1) * days : 2 * (g + 1) * days, :] = cross[g * days : (g + 1) * days, half:]

    grp_b[me_g] = own_b[pl.ds(pl.multiple_of(core * (own_b.shape[0] // CORES), SUB), own_b.shape[0] // CORES), :]
    cell_b[me_c] = sum_slots(b1, grp_b)
    b2 = spread(cell_b, me_c, cell_peers, zb_send, zb_recv)
    sum_grps(c1, own_c, grp_c, cell_c)
    c2 = spread(cell_c, me_c, cell_peers, zc_send, zc_recv)

    def both(copies, slots, target, index):
        target[core] = sum_slots(copies, slots)
        return send(target.at[core], target.at[core], core_send.at[index], core_recv.at[index], {"grp": other})

    a3 = both(a2, chip_a, all_a, 2)
    ones_ref[...] = jnp.ones_like(ones_ref)
    b3 = both(b2, cell_b, all_b, 3)
    x1 = to_grps(own_x, grp_x, gx_send, gx_recv)

    a3.wait_recv()
    packed = jnp.concatenate([all_a[i] for i in range(CORES)], axis=0)
    first = jnp.concatenate([packed[:, :quarter], packed[:, quarter:]], axis=0)
    row0, col0, back0 = scales(first)
    r_00, w_00 = factor_base(first * col0 * row0, ones_ref)

    count = own_c.shape[0] // grps
    all_c[pl.ds(pl.multiple_of(me_g * count, SUB), count), :] = sum_slots(c2, cell_c)
    c3 = [
        send(rows_of(all_c, me_g, count), rows_of(all_c, me_g, count), ac_send.at[i], ac_recv.at[i], peer)
        for i, peer in enumerate(grp_peers)]

    b3.wait_recv()
    packed = jnp.concatenate([all_b[i] for i in range(CORES)], axis=0)
    row1, col1, back1 = scales(packed[:, quarter:])
    r11, w11 = extend(
        r_00, w_00, packed[:, :quarter] * col0 * row1, packed[:, quarter:] * col1 * row1, ones_ref)
    left_row, left_col = jnp.concatenate([row0, row1], axis=1), jnp.concatenate([col0, col1], axis=0)
    zero = jnp.zeros((half, half), jnp.float32)
    r_ref[0:half, 0:half] = r11 * jnp.concatenate([back0, back1], axis=1)
    r_ref[half:, 0:half] = zero
    inv_ref[0:half, 0:half] = w11 * left_row
    inv_ref[0:half, half:] = zero

    sum_grps(x1, own_x, grp_x, cell_x)
    x2 = spread(cell_x, me_c, cell_peers, zx_send, zx_recv)

    for copy in c3:
        copy.wait_recv()
    upper = all_c[half : half + quarter, :]
    last = all_c[half + quarter : half + quarter + eighth, :]
    last = jnp.concatenate([last[:, :quarter], last[:, quarter:]], axis=0)
    row2, col2, back2 = scales(upper[:, :quarter])
    row3, col3, back3 = scales(last)
    right_row, back = jnp.concatenate([row2, row3], axis=1), jnp.concatenate([back2, back3], axis=1)
    r12 = dot(w11, all_c[0:half, :] * left_col * right_row, ((1,), (0,)), HIGHEST)
    r21 = r12.T
    taken = dot(r21, r12, ((1,), (0,)), HIGHEST)
    upper = upper * col2 * right_row - taken[:quarter]
    last = last * col3 * row3 - taken[quarter:, quarter:]
    mixed = dot(r21, w11, ((1,), (0,)), HIGHEST)
    r_ref[0:half, half:] = r12 * back
    r_00, w_00 = factor_base(upper[:, :quarter], ones_ref)
    r22, w22 = extend(r_00, w_00, upper[:, quarter:], last, ones_ref)
    r_ref[half:, half:] = r22 * back
    inv_ref[half:, 0:half] = -dot(w22, mixed, ((1,), (0,)), HIGHEST) * left_row
    inv_ref[half:, half:] = w22 * right_row
    cross_ref[...] = sum_slots(x2, cell_x)
    for copy in started:
        copy.wait_send()


def factored(sketch, slab, cells, grps):
    k, days = sketch.shape[1], slab.shape[1]
    half, quarter = k // 2, k // 4
    chips = cells * grps // CORES
    f32 = jnp.float32
    dma = pltpu.SemaphoreType.DMA
    a_rows, b_rows, x_rows = quarter // 2, quarter, 2 * days
    c_rows = pl.cdiv(half + quarter + quarter // 2, SUB * grps) * SUB * grps
    assert grps % CORES == 0 and cells > 1 and k % (8 * SUB) == 0
    assert x_rows % (2 * SUB * grps) == 0

    def small(rows):
        part = rows // CORES
        return [pltpu.VMEM((rows, half), f32), pltpu.VMEM((part, half), f32),
                pltpu.VMEM((chips, part, half), f32), pltpu.VMEM((CORES, part, half), f32)]

    def large(rows):
        part = rows // grps
        return [pltpu.VMEM((rows, half), f32), pltpu.VMEM((grps - 1, part, half), f32),
                pltpu.VMEM((cells, part, half), f32)]

    return pl.pallas_call(
        functools.partial(factor_kernel, cells, grps),
        out_shape=(
            jax.ShapeDtypeStruct((k, k), f32),
            jax.ShapeDtypeStruct((k, k), f32),
            jax.ShapeDtypeStruct((x_rows // grps, half), f32),
            jax.ShapeDtypeStruct(sketch.shape, sketch.dtype),
        ),
        in_specs=[pl.BlockSpec(memory_space=pltpu.HBM)] * 2,
        out_specs=(pl.BlockSpec(memory_space=pltpu.VMEM),) * 4,
        scratch_shapes=[
            pltpu.VMEM(slab.shape, slab.dtype),
            dma((len(chunks_of(sketch.shape[0], SUM_STEP)),)),
            dma((len(chunks_of(slab.shape[0], SUM_STEP)),)),
            pltpu.VMEM((SUB, k), f32),
        ] + small(a_rows) + [
            pltpu.VMEM((b_rows, half), f32),
            pltpu.VMEM((grps, b_rows // CORES, half), f32),
            pltpu.VMEM((cells, b_rows // CORES, half), f32),
            pltpu.VMEM((CORES, b_rows // CORES, half), f32),
        ] + large(c_rows) + [pltpu.VMEM((c_rows, half), f32)] + large(x_rows)
        + [dma((4,))] * 2 + [dma((chips - 1,))] * 2 + [dma((grps - 1,))] * 2 + [dma((cells - 1,))] * 2
        + [dma((grps - 1,))] * 2 + [dma((cells - 1,))] * 2 + [dma((grps - 1,))] * 4 + [dma((cells - 1,))] * 2,
        compiler_params=pltpu.CompilerParams(collective_id=0, has_side_effects=True, vmem_limit_bytes=VMEM_LIMIT),
        name="reduce_and_factor",
    )(pltpu.with_memory_space_constraint(sketch, pltpu.HBM), pltpu.with_memory_space_constraint(slab, pltpu.HBM))


def basis_kernel(
    r_in, inv_ref, cross_ref, sketch_ref, r_hbm, basis_hbm, proj_ref, basis_ref, r_sem, store_sems,
):
    steps = chunks_of(sketch_ref.shape[0], BASIS_STEP)
    half = cross_ref.shape[1]
    days = cross_ref.shape[0] // 2
    stores = [pltpu.make_async_copy(r_in, r_hbm, r_sem)]
    stores[0].start()
    whole = inv_ref[...]
    high = whole.astype(jnp.bfloat16)
    low = (whole - high.astype(jnp.float32)).astype(jnp.bfloat16)
    for i, rows in enumerate(steps):
        part = sketch_ref[rows, :]
        exact = dot(part, high, ((1,), (1,))) + dot(part, low, ((1,), (1,)))
        basis_ref[rows, :] = exact.astype(jnp.bfloat16)
        stores.append(pltpu.make_async_copy(basis_ref.at[rows, :], basis_hbm.at[rows, :], store_sems.at[i]))
        stores[-1].start()
    count = proj_ref.shape[1]
    mine = inv_ref[pl.ds(pl.multiple_of(lax.axis_index("cell") * count, SUB), count), :]
    proj_ref[...] = dot(cross_ref[0:days, :], mine[:, :half], ((1,), (1,)), HIGHEST) + dot(
        cross_ref[days:, :], mine[:, half:], ((1,), (1,)), HIGHEST)
    for store in stores:
        store.wait()


def local(cells, grps, sketch, slab):
    k, days = sketch.shape[1], slab.shape[1]
    r_in, inverse, cross, held = factored(sketch, slab, cells, grps)
    vmem = pl.BlockSpec(memory_space=pltpu.VMEM)
    hbm = pl.BlockSpec(memory_space=pl.ANY)
    steps = len(chunks_of(sketch.shape[0], BASIS_STEP))
    r_factor, basis, projected = pl.pallas_call(
        basis_kernel,
        out_shape=(
            jax.ShapeDtypeStruct((k, k), jnp.float32),
            jax.ShapeDtypeStruct(sketch.shape, jnp.bfloat16),
            jax.ShapeDtypeStruct((days // grps, k // cells), jnp.float32),
        ),
        in_specs=[vmem] * 4,
        out_specs=(hbm, hbm, vmem),
        scratch_shapes=[
            pltpu.VMEM(sketch.shape, jnp.bfloat16),
            pltpu.SemaphoreType.DMA,
            pltpu.SemaphoreType.DMA((steps,)),
        ],
        compiler_params=pltpu.CompilerParams(vmem_limit_bytes=VMEM_LIMIT),
        name="basis",
    )(r_in, inverse, cross, held)
    return r_factor, basis, projected.T


def solution(mesh):
    cells, grps = mesh.shape["cell"], mesh.shape["grp"]
    in_specs = (P(("parts", "cell", "grp"), None), P(("parts", "cell", "grp"), None))
    out_specs = (P("parts", None), P(("parts", "cell", "grp"), None), P(("parts", "cell"), "grp"))
    return jax.shard_map(
        functools.partial(local, cells, grps), mesh=mesh, in_specs=in_specs, out_specs=out_specs, check_vma=False)
```

```python
import functools

import jax
import jax.numpy as jnp
from jax import lax
from jax.experimental import pallas as pl
from jax.experimental.pallas import tpu as pltpu
from jax.sharding import PartitionSpec as P

SUB = 8
CORES = 2
VMEM_LIMIT = 20 * 2**20
SUM_STEP = 768
BASIS_STEP = 384
HIGHEST = lax.Precision.HIGHEST


def dot(a, b, contract, precision=None):
    return lax.dot_general(
        a, b, (contract, ((), ())), precision=precision, preferred_element_type=jnp.float32
    )


def chunks_of(total, step):
    return [pl.ds(start, min(step, total - start)) for start in range(0, total, step)]


def sums_over(a_ref, b_ref, loads):
    total = None
    for rows, load in loads:
        load.wait()
        part = dot(a_ref[rows, :], b_ref[rows, :], ((0,), (0,)))
        total = part if total is None else total + part
    return total


def tree(terms):
    terms=list(terms)
    while len(terms) > 1:
        terms = [a + b for a, b in zip(terms[::2], terms[1::2])] + terms[len(terms) // 2 * 2 :]
    return terms[0]

def factor_base(block, ones_ref):
    n = block.shape[0]
    shape = (SUB, 2 * n)
    ones = ones_ref[:, : 2 * n]
    tiles = n // SUB
    sub = lax.broadcasted_iota(jnp.int32, shape, 0)
    lane = lax.broadcasted_iota(jnp.int32, shape, 1)
    eye = jnp.where(
        lax.broadcasted_iota(jnp.int32, (n, n), 0) == lax.broadcasted_iota(jnp.int32, (n, n), 1), 1.0, 0.0)
    wide = jnp.concatenate([block, eye.astype(jnp.float32)], axis=1)
    m = [wide[q * SUB : (q + 1) * SUB, :] for q in range(tiles)]
    done = []
    ahead = None

    def row(x, j):
        return jnp.broadcast_to(x[j : j + 1, :], shape)

    def col(x, j):
        return jnp.broadcast_to(x[:, j : j + 1], shape)

    for p in range(tiles):
        t = m[p]
        c = [col(t, p * SUB + i) * ones for i in range(0 if ahead is None else 2, SUB)]
        c = c if ahead is None else ahead + c
        after = m[p + 1] if p + 1 < tiles else None
        if after is not None:
            e = [col(after, p * SUB + i) * ones for i in range(SUB)]
            ahead = [col(after, (p + 1) * SUB + i) * ones for i in range(2)]
        corner = [row(c[0], 0), row(c[1], 0), row(c[1], 1)]
        r = jnp.zeros(shape, jnp.float32)
        for j in range(0, SUB, 2):
            k = j + 1
            at_j, at_k = sub == j, sub == k
            pair = at_j | at_k
            a, b, d = corner
            det = a * d - b * b
            inv = 1.0 / det
            root_a, root = lax.rsqrt(a), lax.rsqrt(det)
            f_j = jnp.where(at_j, -d, jnp.where(at_k, b, c[j] * d - c[k] * b))
            f_k = jnp.where(at_j, b, jnp.where(at_k, -a, c[k] * a - c[j] * b))
            t_j, t_k = row(t, j), row(t, k)
            r = jnp.where(at_j, t_j * root_a, jnp.where(at_k, (t_k * a - t_j * b) * (root_a * root), r))
            t = jnp.where(pair, 0.0, t) - (f_j * t_j + f_k * t_k) * inv
            if after is not None:
                n_j, n_k = e[j] * d - e[k] * b, e[k] * a - e[j] * b
                ahead = [x - (n_j * row(e[j], i) + n_k * row(e[k], i)) * inv for i, x in enumerate(ahead)]
            if k + 1 < SUB:
                s_j = {i: row(c[i], j) for i in range(k + 1, SUB)}
                s_k = {i: row(c[i], k) for i in range(k + 1, SUB)}
                x, y = k + 1, k + 2
                v = {h: (s_j[h] * d - s_k[h] * b, s_k[h] * a - s_j[h] * b) for h in (x, y)}
                corner = [
                    row(c[i], h) - (v[h][0] * s_j[i] + v[h][1] * s_k[i]) * inv for h, i in ((x, x), (x, y), (y, y))]
                for i in range(k + 1, SUB):
                    c[i] = jnp.where(pair, 0.0, c[i]) - (f_j * s_j[i] + f_k * s_k[i]) * inv
                    if after is not None:
                        e[i] = e[i] - (n_j * s_j[i] + n_k * s_k[i]) * inv
        done.append(jnp.where((lane >= sub + p * SUB), r, 0.0))
        if p + 1 < tiles:
            rows = [row(t, i) for i in range(SUB)]
            later = range(p + 1, tiles)
            terms = [[col(m[q], p * SUB + i) * rows[i] for q in later] for i in range(SUB)]
            for at, q in enumerate(later):
                m[q] = m[q] - tree([terms[i][at] for i in range(SUB)])
    done = jnp.concatenate(done, axis=0)
    return done[:, :n], done[:, n:]


def scales(block):
    n = block.shape[0]
    eye = lax.broadcasted_iota(jnp.int32, (n, n), 0) == lax.broadcasted_iota(jnp.int32, (n, n), 1)
    kept = jnp.where(eye, block, 0.0)
    across = jnp.sum(kept, axis=0, keepdims=True)
    row, col = lax.rsqrt(across), lax.rsqrt(jnp.sum(kept, axis=1, keepdims=True))
    return row, col, across * row


def extend(r11, w11, g12, g22, ones_ref):
    h = r11.shape[0]
    r12 = dot(w11, g12, ((1,), (0,)), HIGHEST)
    r21 = r12.T
    r22, w22 = factor_base(g22 - dot(r21, r12, ((1,), (0,)), HIGHEST), ones_ref)
    w21 = -dot(w22, dot(r21, w11, ((1,), (0,)), HIGHEST), ((1,), (0,)), HIGHEST)
    zero = jnp.zeros((h, h), jnp.float32)
    return (
        jnp.concatenate([jnp.concatenate([r11, r12], axis=1), jnp.concatenate([zero, r22], axis=1)], axis=0),
        jnp.concatenate([jnp.concatenate([w11, zero], axis=1), jnp.concatenate([w21, w22], axis=1)], axis=0),
    )


def factor_kernel(
    cells, grps, sketch_hbm, slab_hbm, r_ref, inv_ref, cross_ref, sketch_ref,
    slab_ref, sketch_sems, slab_sems, ones_ref,
    own_a, core_a, chip_a, all_a, own_b, grp_b, cell_b, all_b,
    own_c, grp_c, cell_c, all_c, own_x, grp_x, cell_x,
    core_send, core_recv, a_send, a_recv, gb_send, gb_recv, zb_send, zb_recv, gc_send, gc_recv, zc_send, zc_recv,
    ac_send, ac_recv, gx_send, gx_recv, zx_send, zx_recv,
):
    def loading(source, target, sems):
        loads = []
        for i, rows in enumerate(chunks_of(source.shape[0], SUM_STEP)):
            load = pltpu.make_async_copy(source.at[rows, :], target.at[rows, :], sems.at[i])
            load.start()
            loads.append((rows, load))
        return loads

    sketch_loads = loading(sketch_hbm, sketch_ref, sketch_sems)
    me_c = lax.axis_index("cell")
    me_g = lax.axis_index("grp")
    chips_x = grps // CORES
    me_x, core = lax.div(me_g, CORES), lax.rem(me_g, CORES)
    me_chip = me_c * chips_x + me_x
    other = me_x * CORES + (1 - core)
    half = own_b.shape[1]
    quarter = half // 2
    started = []

    def send(source, target, send_sem, recv_sem, device):
        copy = pltpu.make_async_remote_copy(
            src_ref=source, dst_ref=target, send_sem=send_sem, recv_sem=recv_sem,
            device_id=device, device_id_type=pl.DeviceIdType.MESH)
        copy.start()
        started.append(copy)
        return copy

    def rows_of(ref, index, count):
        return ref.at[pl.ds(pl.multiple_of(index * count, SUB), count), :]

    grp_peers = [{"grp": lax.rem(me_g + d, grps)} for d in range(1, grps)]
    cell_peers = [{"cell": lax.rem(me_c + d, cells)} for d in range(1, cells)]
    chip_peers = [
        {"cell": lax.rem(me_c + dc, cells), "grp": lax.rem(me_x + dx, chips_x) * CORES + core}
        for dx in reversed(range(chips_x)) for dc in sorted(range(cells), key=lambda d: -min(d, cells - d)) if dc or dx]

    barrier = pltpu.get_barrier_semaphore()
    beyond = [{"cell": peer["cell"], "grp": peer["grp"]} for peer in chip_peers]
    for peer in beyond + [p for d, p in enumerate(grp_peers, 1)]:
        pl.semaphore_signal(barrier, inc=1, device_id=peer, device_id_type=pl.DeviceIdType.MESH)

    gram = sums_over(sketch_ref, sketch_ref, sketch_loads)
    slab_loads = loading(slab_hbm, slab_ref, slab_sems)
    eighth = quarter // 2
    own_a[...] = jnp.concatenate([gram[:eighth, :quarter], gram[eighth:quarter, :quarter]], axis=1)
    own_b[...] = jnp.concatenate([gram[:quarter, quarter:half], gram[quarter:half, quarter:half]], axis=1)
    pl.semaphore_wait(barrier, len(beyond) + len(grp_peers))

    def halves(own, landing, index):
        count = own.shape[0] // CORES
        return send(rows_of(own, 1 - core, count), landing, core_send.at[index], core_recv.at[index], {"grp": other})

    a1 = halves(own_a, core_a, 0)
    count = own_b.shape[0] // CORES
    b1 = [
        send(rows_of(own_b, lax.rem(peer["grp"], CORES), count), grp_b.at[me_g], gb_send.at[i], gb_recv.at[i], peer)
        for i, peer in enumerate(grp_peers)]
    own_c[0:half, :] = gram[:half, half:]
    own_c[half : half + quarter, :] = gram[half : half + quarter, half:]
    last = gram[half + quarter :, half + quarter :]
    own_c[half + quarter : half + quarter + eighth, :] = jnp.concatenate([last[:eighth], last[eighth:]], axis=1)
    spare = own_c.shape[0] - half - quarter - eighth
    if spare:
        own_c[half + quarter + eighth :, :] = jnp.zeros((spare, half), jnp.float32)

    def to_grps(own, landing, send_sems, recv_sems):
        count = own.shape[0] // grps
        return [
            send(rows_of(own, peer["grp"], count), landing.at[i], send_sems.at[i], recv_sems.at[i], peer)
            for i, peer in enumerate(grp_peers)]

    def sum_grps(copies, own, landing, slots):
        count = own.shape[0] // grps
        for copy in copies:
            copy.wait_recv()
        slots[me_c] = tree([own[pl.ds(pl.multiple_of(me_g * count, SUB), count), :]] + [landing[i] for i in range(grps - 1)])

    def spread(slots, me, peers, send_sems, recv_sems):
        return [send(slots.at[me], slots.at[me], send_sems.at[i], recv_sems.at[i], peer) for i, peer in enumerate(peers)]

    def sum_slots(copies, slots):
        for copy in copies:
            copy.wait_recv()
        return tree([slots[i] for i in range(slots.shape[0])])

    c1 = to_grps(own_c, grp_c, gc_send, gc_recv)

    def chip_sum(copy, own, landing, slots, send_sems, recv_sems):
        count = own.shape[0] // CORES
        copy.wait_recv()
        slots[me_chip] = own[pl.ds(pl.multiple_of(core * count, SUB), count), :] + landing[...]
        return spread(slots, me_chip, chip_peers, send_sems, recv_sems)

    a2 = chip_sum(a1, own_a, core_a, chip_a, a_send, a_recv)

    cross = sums_over(slab_ref, sketch_ref, slab_loads)
    days = cross.shape[0] // grps
    for g in range(grps):
        own_x[2 * g * days : (2 * g + 1) * days, :] = cross[g * days : (g + 1) * days, :half]
        own_x[(2 * g + 1) * days : 2 * (g + 1) * days, :] = cross[g * days : (g + 1) * days, half:]

    grp_b[me_g] = own_b[pl.ds(pl.multiple_of(core * (own_b.shape[0] // CORES), SUB), own_b.shape[0] // CORES), :]
    cell_b[me_c] = sum_slots(b1, grp_b)
    b2 = spread(cell_b, me_c, cell_peers, zb_send, zb_recv)
    sum_grps(c1, own_c, grp_c, cell_c)
    c2 = spread(cell_c, me_c, cell_peers, zc_send, zc_recv)

    def both(copies, slots, target, index):
        target[core] = sum_slots(copies, slots)
        return send(target.at[core], target.at[core], core_send.at[index], core_recv.at[index], {"grp": other})

    a3 = both(a2, chip_a, all_a, 2)
    ones_ref[...] = jnp.ones_like(ones_ref)
    b3 = both(b2, cell_b, all_b, 3)
    x1 = to_grps(own_x, grp_x, gx_send, gx_recv)

    a3.wait_recv()
    packed = jnp.concatenate([all_a[i] for i in range(CORES)], axis=0)
    first = jnp.concatenate([packed[:, :quarter], packed[:, quarter:]], axis=0)
    row0, col0, back0 = scales(first)
    r_00, w_00 = factor_base(first * col0 * row0, ones_ref)

    count = own_c.shape[0] // grps
    all_c[pl.ds(pl.multiple_of(me_g * count, SUB), count), :] = sum_slots(c2, cell_c)
    c3 = [
        send(rows_of(all_c, me_g, count), rows_of(all_c, me_g, count), ac_send.at[i], ac_recv.at[i], peer)
        for i, peer in enumerate(grp_peers)]

    b3.wait_recv()
    packed = jnp.concatenate([all_b[i] for i in range(CORES)], axis=0)
    row1, col1, back1 = scales(packed[:, quarter:])
    r11, w11 = extend(
        r_00, w_00, packed[:, :quarter] * col0 * row1, packed[:, quarter:] * col1 * row1, ones_ref)
    left_row, left_col = jnp.concatenate([row0, row1], axis=1), jnp.concatenate([col0, col1], axis=0)
    zero = jnp.zeros((half, half), jnp.float32)
    r_ref[0:half, 0:half] = r11 * jnp.concatenate([back0, back1], axis=1)
    r_ref[half:, 0:half] = zero
    inv_ref[0:half, 0:half] = w11 * left_row
    inv_ref[0:half, half:] = zero

    sum_grps(x1, own_x, grp_x, cell_x)
    x2 = spread(cell_x, me_c, cell_peers, zx_send, zx_recv)

    for copy in c3:
        copy.wait_recv()
    upper = all_c[half : half + quarter, :]
    last = all_c[half + quarter : half + quarter + eighth, :]
    last = jnp.concatenate([last[:, :quarter], last[:, quarter:]], axis=0)
    row2, col2, back2 = scales(upper[:, :quarter])
    row3, col3, back3 = scales(last)
    right_row, back = jnp.concatenate([row2, row3], axis=1), jnp.concatenate([back2, back3], axis=1)
    r12 = dot(w11, all_c[0:half, :] * left_col * right_row, ((1,), (0,)), HIGHEST)
    r21 = r12.T
    taken = dot(r21, r12, ((1,), (0,)), HIGHEST)
    upper = upper * col2 * right_row - taken[:quarter]
    last = last * col3 * row3 - taken[quarter:, quarter:]
    mixed = dot(r21, w11, ((1,), (0,)), HIGHEST)
    r_ref[0:half, half:] = r12 * back
    r_00, w_00 = factor_base(upper[:, :quarter], ones_ref)
    r22, w22 = extend(r_00, w_00, upper[:, quarter:], last, ones_ref)
    r_ref[half:, half:] = r22 * back
    inv_ref[half:, 0:half] = -dot(w22, mixed, ((1,), (0,)), HIGHEST) * left_row
    inv_ref[half:, half:] = w22 * right_row
    cross_ref[...] = sum_slots(x2, cell_x)
    for copy in started:
        copy.wait_send()


def factored(sketch, slab, cells, grps):
    k, days = sketch.shape[1], slab.shape[1]
    half, quarter = k // 2, k // 4
    chips = cells * grps // CORES
    f32 = jnp.float32
    dma = pltpu.SemaphoreType.DMA
    a_rows, b_rows, x_rows = quarter // 2, quarter, 2 * days
    c_rows = pl.cdiv(half + quarter + quarter // 2, SUB * grps) * SUB * grps
    assert grps % CORES == 0 and cells > 1 and k % (8 * SUB) == 0
    assert x_rows % (2 * SUB * grps) == 0

    def small(rows):
        part = rows // CORES
        return [pltpu.VMEM((rows, half), f32), pltpu.VMEM((part, half), f32),
                pltpu.VMEM((chips, part, half), f32), pltpu.VMEM((CORES, part, half), f32)]

    def large(rows):
        part = rows // grps
        return [pltpu.VMEM((rows, half), f32), pltpu.VMEM((grps - 1, part, half), f32),
                pltpu.VMEM((cells, part, half), f32)]

    return pl.pallas_call(
        functools.partial(factor_kernel, cells, grps),
        out_shape=(
            jax.ShapeDtypeStruct((k, k), f32),
            jax.ShapeDtypeStruct((k, k), f32),
            jax.ShapeDtypeStruct((x_rows // grps, half), f32),
            jax.ShapeDtypeStruct(sketch.shape, sketch.dtype),
        ),
        in_specs=[pl.BlockSpec(memory_space=pltpu.HBM)] * 2,
        out_specs=(pl.BlockSpec(memory_space=pltpu.VMEM),) * 4,
        scratch_shapes=[
            pltpu.VMEM(slab.shape, slab.dtype),
            dma((len(chunks_of(sketch.shape[0], SUM_STEP)),)),
            dma((len(chunks_of(slab.shape[0], SUM_STEP)),)),
            pltpu.VMEM((SUB, k), f32),
        ] + small(a_rows) + [
            pltpu.VMEM((b_rows, half), f32),
            pltpu.VMEM((grps, b_rows // CORES, half), f32),
            pltpu.VMEM((cells, b_rows // CORES, half), f32),
            pltpu.VMEM((CORES, b_rows // CORES, half), f32),
        ] + large(c_rows) + [pltpu.VMEM((c_rows, half), f32)] + large(x_rows)
        + [dma((4,))] * 2 + [dma((chips - 1,))] * 2 + [dma((grps - 1,))] * 2 + [dma((cells - 1,))] * 2
        + [dma((grps - 1,))] * 2 + [dma((cells - 1,))] * 2 + [dma((grps - 1,))] * 4 + [dma((cells - 1,))] * 2,
        compiler_params=pltpu.CompilerParams(collective_id=0, has_side_effects=True, vmem_limit_bytes=VMEM_LIMIT),
        name="reduce_and_factor",
    )(pltpu.with_memory_space_constraint(sketch, pltpu.HBM), pltpu.with_memory_space_constraint(slab, pltpu.HBM))


def basis_kernel(
    r_in, inv_ref, cross_ref, sketch_ref, r_hbm, basis_hbm, proj_ref, basis_ref, r_sem, store_sems,
):
    steps = chunks_of(sketch_ref.shape[0], BASIS_STEP)
    half = cross_ref.shape[1]
    days = cross_ref.shape[0] // 2
    stores = [pltpu.make_async_copy(r_in, r_hbm, r_sem)]
    stores[0].start()
    whole = inv_ref[...]
    high = whole.astype(jnp.bfloat16)
    low = (whole - high.astype(jnp.float32)).astype(jnp.bfloat16)
    for i, rows in enumerate(steps):
        part = sketch_ref[rows, :]
        exact = dot(part, high, ((1,), (1,))) + dot(part, low, ((1,), (1,)))
        basis_ref[rows, :] = exact.astype(jnp.bfloat16)
        stores.append(pltpu.make_async_copy(basis_ref.at[rows, :], basis_hbm.at[rows, :], store_sems.at[i]))
        stores[-1].start()
    count = proj_ref.shape[1]
    mine = inv_ref[pl.ds(pl.multiple_of(lax.axis_index("cell") * count, SUB), count), :]
    proj_ref[...] = dot(cross_ref[0:days, :], mine[:, :half], ((1,), (1,)), HIGHEST) + dot(
        cross_ref[days:, :], mine[:, half:], ((1,), (1,)), HIGHEST)
    for store in stores:
        store.wait()


def local(cells, grps, sketch, slab):
    k, days = sketch.shape[1], slab.shape[1]
    r_in, inverse, cross, held = factored(sketch, slab, cells, grps)
    vmem = pl.BlockSpec(memory_space=pltpu.VMEM)
    hbm = pl.BlockSpec(memory_space=pl.ANY)
    steps = len(chunks_of(sketch.shape[0], BASIS_STEP))
    r_factor, basis, projected = pl.pallas_call(
        basis_kernel,
        out_shape=(
            jax.ShapeDtypeStruct((k, k), jnp.float32),
            jax.ShapeDtypeStruct(sketch.shape, jnp.bfloat16),
            jax.ShapeDtypeStruct((days // grps, k // cells), jnp.float32),
        ),
        in_specs=[vmem] * 4,
        out_specs=(hbm, hbm, vmem),
        scratch_shapes=[
            pltpu.VMEM(sketch.shape, jnp.bfloat16),
            pltpu.SemaphoreType.DMA,
            pltpu.SemaphoreType.DMA((steps,)),
        ],
        compiler_params=pltpu.CompilerParams(vmem_limit_bytes=VMEM_LIMIT),
        name="basis",
    )(r_in, inverse, cross, held)
    return r_factor, basis, projected.T


def solution(mesh):
    cells, grps = mesh.shape["cell"], mesh.shape["grp"]
    in_specs = (P(("parts", "cell", "grp"), None), P(("parts", "cell", "grp"), None))
    out_specs = (P("parts", None), P(("parts", "cell", "grp"), None), P(("parts", "cell"), "grp"))
    return jax.shard_map(
        functools.partial(local, cells, grps), mesh=mesh, in_specs=in_specs, out_specs=out_specs, check_vma=False)
```
